128 devices in a mesh: box: 64 (over z, y, x), col: 2 (over core).
Axes of the slice: x: 4, y: 4, z: 4, core: 2. Of those that a mesh axis runs over, the one named last changes fastest.
Arguments:
- points: bfloat16 [1024, 3, 512], P('box'), may hold values from 0 to 1
- sketch: bfloat16 [1024, 512, 128], P('box', 'col'), may hold values from -6 to 6
- near_mask: int32 [1024, 9], P('box'), may hold values from 0 to 1, as said below
Outputs:
- basis: bfloat16 [1024, 512, 128], P('box', 'col')
- coupling: float32 [1024, 9, 128, 128], P('box', None, 'col')
The draws below stay inside these ranges and needn't reach their ends.
Inputs may be any that keep to these rules, and one draw needn't show every extreme that they name: near_mask[b, s] is 1 for the box itself and for its edge neighbours that lie on the plate, 0 for slots off the plate; a diagonal neighbour is near or not by a relation that is symmetric between the two boxes.
All inputs are finite; a program needn't handle non-finite values.
Results may differ from the reference program's by a relative error of at most 0.007.
Values may be sent and summed in bfloat16 or wider, within the bound.
A program may use at most 64 MiB of HBM per device.

```python
import math
import jax
import jax.numpy as jnp
from jax import lax

M = 512
R = 128
TILE = 4
DGRID = 8
NB = 1024


def draw_near_mask(key, part):
    plate_side = TILE * DGRID
    diag_down = jax.random.randint(jax.random.fold_in(key, 11), (plate_side, plate_side), 0, 2)
    diag_up = jax.random.randint(jax.random.fold_in(key, 12), (plate_side, plate_side), 0, 2)
    middle = plate_side // 2
    grid_rows = jnp.arange(plate_side)[:, None]
    grid_cols = jnp.arange(plate_side)[None, :]
    force_down = (grid_rows == middle) & (grid_cols == middle) | (grid_rows == middle - 1) & (grid_cols == middle - 1)
    force_up = (grid_rows == middle) & (grid_cols == middle - 1) | (grid_rows == middle - 1) & (grid_cols == middle)
    diag_down = jnp.where(force_down, 1, diag_down)
    diag_up = jnp.where(force_up, 1, diag_up)
    box_ids = jnp.arange(NB, dtype=jnp.int32)
    group_ids = box_ids // (TILE * TILE)
    local_ids = box_ids % (TILE * TILE)
    grid_y = group_ids // DGRID * TILE + local_ids // TILE
    grid_x = group_ids % DGRID * TILE + local_ids % TILE
    columns = []
    for stencil in range(9):
        offset_y = stencil // 3 - 1
        offset_x = stencil % 3 - 1
        near_y = grid_y + offset_y
        near_x = grid_x + offset_x
        inside = (near_y >= 0) & (near_y < plate_side) & (near_x >= 0) & (near_x < plate_side)
        if offset_y == 0 or offset_x == 0:
            allowed = inside
        else:
            low_y = jnp.clip(jnp.minimum(grid_y, near_y), 0, plate_side - 1)
            low_x = jnp.clip(jnp.minimum(grid_x, near_x), 0, plate_side - 1)
            bit_table = diag_down if offset_y == offset_x else diag_up
            allowed = inside & (bit_table[low_y, low_x] == 1)
        columns.append(allowed.astype(jnp.int32))
    return jnp.stack(columns, axis=1)


def shard_levels(own_key, shape, pieces, smallest, top_value):
    def one(dim, shards_of):
        steps = jax.random.uniform(jax.random.fold_in(jax.random.fold_in(own_key, 6), dim), (shards_of,), jnp.float32, smallest / len(pieces), top_value / len(pieces))
        return jnp.repeat(jnp.exp(steps), shape[dim] // shards_of).reshape((-1,) + (1,) * (len(shape) - dim - 1))

    loudness = one(*pieces[0])
    for cut in pieces[1:]:
        loudness = loudness * one(*cut)
    return loudness


def normal_values(own_key, dims, width, reach, pieces=(), kind=jnp.bfloat16):
    factor_of = shard_levels(own_key, dims, pieces, -0.22, 0.18) if pieces else 1.0
    entries = jax.random.normal(own_key, dims, jnp.float32) * width * factor_of
    return jnp.minimum(jnp.maximum(entries, -reach), reach).astype(kind)


def setup_inputs(seed: int = 0) -> dict:
    streams_of = jax.random.split(jax.random.key(seed), 4)
    points = jnp.clip(1.0 * jax.random.uniform(streams_of[0], (NB, 3, M), jnp.float32) ** shard_levels(streams_of[0], (NB, 3, M), ((0, 64),), -0.2, 0.2), 0.0, 1.0).astype(jnp.bfloat16)
    sketch = normal_values(streams_of[1], (NB, M, R), 1.0, 6.0, ((0, 64), (1, 2)))
    near_mask = draw_near_mask(jax.random.fold_in(streams_of[3], 71), 0)
    return dict(points=points, sketch=sketch, near_mask=near_mask)


lift_scale = 0.25

def interaction(row_points, col_points, shift_y, shift_x, first_row, first_col, centre, box_points):
    row_coords = row_points.astype(jnp.float32)
    col_coords = col_points.astype(jnp.float32)
    delta_u = shift_x + col_coords[..., 0, None, :] - row_coords[..., 0, :, None]
    delta_v = shift_y + col_coords[..., 1, None, :] - row_coords[..., 1, :, None]
    delta_w = lift_scale * (col_coords[..., 2, None, :] - row_coords[..., 2, :, None])
    strength = 0.25 / math.sqrt(box_points)
    soften = 0.5 / math.sqrt(box_points)
    values = strength / jnp.sqrt(delta_u * delta_u + delta_v * delta_v + delta_w * delta_w + soften * soften)
    if centre:
        row_ids = first_row + jnp.arange(row_coords.shape[-1], dtype=jnp.int32)
        col_ids = first_col + jnp.arange(col_coords.shape[-1], dtype=jnp.int32)
        values = values + jnp.where(row_ids[:, None] == col_ids[None, :], 1.0, 0.0).astype(jnp.float32)
    return values

def neighbour_table():
    plate_side = TILE * DGRID
    box_ids = jnp.arange(NB, dtype=jnp.int32)
    group_ids = box_ids // (TILE * TILE)
    local_ids = box_ids % (TILE * TILE)
    grid_y = group_ids // DGRID * TILE + local_ids // TILE
    grid_x = group_ids % DGRID * TILE + local_ids % TILE
    columns = []
    for stencil in range(9):
        near_y = jnp.clip(grid_y + (stencil // 3 - 1), 0, plate_side - 1)
        near_x = jnp.clip(grid_x + (stencil % 3 - 1), 0, plate_side - 1)
        near_ids = (near_y // TILE * DGRID + near_x // TILE) * (TILE * TILE) + near_y % TILE * TILE + near_x % TILE
        columns.append(near_ids.astype(jnp.int32))
    return jnp.stack(columns, axis=1)

def orthonormal(sketch_t):
    gram_sum = jnp.einsum('brm,bsm->brs', sketch_t, sketch_t, precision=lax.Precision.HIGHEST) / sketch_t.shape[2]
    lower_factor = jnp.linalg.cholesky(gram_sum)
    identity = jnp.broadcast_to(jnp.eye(gram_sum.shape[1], dtype=gram_sum.dtype), gram_sum.shape)
    inverse_lower = lax.linalg.triangular_solve(lower_factor, identity, left_side=True, lower=True)
    return jnp.einsum('brs,bsm->brm', inverse_lower, sketch_t, precision=lax.Precision.HIGHEST)

def reference(points, sketch, near_mask):
    table_ids = neighbour_table()
    weights = near_mask.astype(jnp.float32)

    def sketch_box(box_index):
        own_coords = points[box_index]
        running = jnp.zeros((M, R), jnp.float32)
        for stencil in range(9):
            near_box = table_ids[box_index, stencil]
            block_vals = interaction(own_coords, points[near_box], stencil // 3 - 1, stencil % 3 - 1, 0, 0, stencil == 4, M).astype(jnp.bfloat16)
            running = running + jnp.dot(block_vals.astype(jnp.float32), sketch[near_box].astype(jnp.float32), preferred_element_type=jnp.float32) * weights[box_index, stencil]
        return running
    sketched = lax.map(sketch_box, jnp.arange(NB, dtype=jnp.int32))
    sketch_t = orthonormal(orthonormal(jnp.transpose(sketched, (0, 2, 1))))
    basis_t = sketch_t.astype(jnp.bfloat16)

    def couple_box(box_index):
        own_coords = points[box_index]
        collected = []
        for stencil in range(9):
            near_box = table_ids[box_index, stencil]
            block_vals = interaction(own_coords, points[near_box], stencil // 3 - 1, stencil % 3 - 1, 0, 0, stencil == 4, M).astype(jnp.bfloat16)
            projected = jnp.dot(basis_t[box_index].astype(jnp.float32), block_vals.astype(jnp.float32), preferred_element_type=jnp.float32).astype(jnp.bfloat16)
            coupling_term = jnp.dot(projected.astype(jnp.float32), jnp.transpose(basis_t[near_box]).astype(jnp.float32), preferred_element_type=jnp.float32) * (1.0 / M) * weights[box_index, stencil]
            collected.append(coupling_term)
        return jnp.stack(collected, axis=0)
    coupling = lax.map(couple_box, jnp.arange(NB, dtype=jnp.int32))
    return (jnp.transpose(basis_t, (0, 2, 1)), coupling)
```

```python
import functools
import math

import jax
import jax.numpy as jnp
import numpy as np
from jax import lax
from jax.experimental import pallas as pl
from jax.experimental.pallas import tpu as pltpu
from jax.sharding import PartitionSpec as P

MESH = pl.DeviceIdType.MESH
HIGHEST = lax.Precision.HIGHEST
TILE = 4
POINTS = 512
RANK = 128
FEATURES = 16
SLOTS = 9
LIMIT = 63 << 20
PANEL = 16
NT = (((1,), (1,)), ((), ()))
TN = (((0,), (0,)), ((), ()))
DIRECTIONS = [(dy, dx) for dy in (-1, 0, 1) for dx in (-1, 0, 1) if (dy, dx) != (0, 0)]


def slot_scales():
    unit = 2.0**13
    out = np.zeros((SLOTS, FEATURES, 1), np.float32)
    for slot in range(SLOTS):
        y, x = slot // 3 - 1, slot % 3 - 1
        out[slot, :, 0] = (
            [-2 * unit, -2 * unit, -unit / 8] + [unit] * 6
            + [-2 * unit * x, -2 * unit * y, 2 * unit * x, 2 * unit * y, unit * (x * x + y * y), 4.0, 0.0]
        )
    return out


def place(step, side, low, high):
    if step == -1:
        return low
    if step == 1:
        return high
    return slice(1, side + 1)


class Halo:
    def __init__(self, plate):
        self.plate = plate
        box, self.col = lax.axis_index("box"), lax.axis_index("col")
        self.row = box // plate * 2 + self.col
        self.column = box % plate
        self.partner = (box, 1 - self.col)

    def device(self, dy, dx):
        high = self.plate * 2
        row = (self.row + dy + high) % high
        column = (self.column + dx + self.plate) % self.plate
        return (row // 2 * self.plate + column, row % 2)

    def barrier(self):
        sem = pltpu.get_barrier_semaphore()
        for dy, dx in DIRECTIONS:
            pl.semaphore_signal(sem, inc=1, device_id=self.device(dy, dx), device_id_type=MESH)
        pl.semaphore_wait(sem, len(DIRECTIONS))

    def copies(self, ext, send, recv):
        made = []
        for n, (dy, dx) in enumerate(DIRECTIONS):
            made.append(
                pltpu.make_async_remote_copy(
                    src_ref=ext.at[place(dy, 2, 1, 2), place(dx, TILE, 1, TILE)],
                    dst_ref=ext.at[place(dy, 2, 3, 0), place(dx, TILE, TILE + 1, 0)],
                    send_sem=send.at[n],
                    recv_sem=recv.at[n],
                    device_id=self.device(dy, dx),
                    device_id_type=MESH,
                )
            )
        return made


def parts(value, count):
    made = []
    for _ in range(count):
        made.append(value.astype(jnp.bfloat16))
        value = value - made[-1].astype(jnp.float32)
    return made


def features(points_ref, row):
    wide = points_ref.astype(jnp.float32)
    u, v, h = wide[0:1], wide[1:2], wide[2:3]
    pieces = parts(u * u + v * v + h * h * 0.0625, 3)
    at = lax.broadcasted_iota(jnp.int32, (FEATURES, POINTS), 0)
    shifted, first = (9, 3) if row else (11, 6)
    out = jnp.where(at == FEATURES - 1, 0.0, 1.0)
    for place_of, value in ((0, u), (shifted, u), (1, v), (shifted + 1, v), (2, h)):
        out = jnp.where(at == place_of, value, out)
    for n in range(3):
        out = jnp.where(at == first + n, pieces[n].astype(jnp.float32), out)
    return out


def eliminate(a_ref, p_ref, panel_ref):
    boxes, rank = a_ref.shape[0], a_ref.shape[1]
    lane = lax.broadcasted_iota(jnp.int32, (boxes, rank), 1)
    row_id = lax.broadcasted_iota(jnp.int32, (rank, rank), 0)
    col_id = lax.broadcasted_iota(jnp.int32, (rank, rank), 1)

    def panel(n, carry):
        first = pl.multiple_of(n * PANEL, PANEL)
        for b in range(boxes):
            panel_ref[:, b, :] = a_ref[b, pl.ds(first, PANEL), :]
        rows = [panel_ref[i] for i in range(PANEL)]
        for k in range(PANEL):
            here = lane == first + k
            index = jnp.full((boxes, rank), first + k, jnp.int32)
            pivot = jnp.take_along_axis(rows[k], index, axis=1)
            inverse = 1.0 / pivot
            scaled = jnp.where(here, inverse, rows[k] * inverse)
            for i in range(k + 1, PANEL):
                factor = jnp.take_along_axis(rows[i], index, axis=1)
                rows[i] = jnp.where(here, 0.0, rows[i]) - factor * scaled
            keep = (lane < first + k) | (lane >= first + PANEL)
            rows[k] = jnp.where(keep, rows[k], jnp.where(here, 1.0, 0.0)) * lax.rsqrt(pivot)
        for i in range(PANEL):
            panel_ref[i] = rows[i]
        below = row_id >= first + PANEL
        inside = (col_id >= first) & (col_id < first + PANEL)
        for b in range(boxes):
            own = panel_ref[:, b, :]
            p_ref[b, pl.ds(first, PANEL), :] = jnp.where(col_id[:PANEL] <= row_id[:PANEL] + first, own, 0.0)
            w1, w2, w3 = parts(own, 3)
            left = jnp.concatenate([w1, w1, w2, w1, w2, w3], 0)
            right = jnp.concatenate([w1, w2, w1, w3, w2, w1], 0)
            update = lax.dot_general(left, right, TN, preferred_element_type=jnp.float32)
            old = a_ref[b]
            a_ref[b] = jnp.where(below, jnp.where(inside, 0.0, old) - update, old)
        return carry

    lax.fori_loop(0, rank // PANEL, panel, 0)


def kernel(
    plate, mask_ref, points_ref, sketch_ref, scale_ref, basis_ref, coupling_ref,
    ext_p, ext_e, ext_o, ext_b, kbuf, turned, y_ref, work, a_ref, p_ref, panel_ref, basis_t, stage,
    local_sem, out_sem, swap_send, swap_recv, p_send, p_recv, o_send, o_recv,
    b_send, b_recv, half_send, half_recv, c_send, c_recv,
):
    halo = Halo(plate)
    own, other = halo.col, 1 - halo.col
    half = sketch_ref.shape[1]
    rank_half = coupling_ref.shape[2]
    inner = slice(1, TILE + 1)
    mine = pl.ds(pl.multiple_of(own * half, half), half)
    theirs = pl.ds(pl.multiple_of(other * half, half), half)
    locals_p, locals_o, swaps = [], [], []
    for r in range(2):
        boxes = pl.ds(own * 8 + r * TILE, TILE)
        away = pl.ds(other * 8 + r * TILE, TILE)
        locals_p.append(pltpu.make_async_copy(points_ref.at[boxes], ext_p.at[1 + r, inner], local_sem.at[r]))
        locals_o.append(
            pltpu.make_async_copy(sketch_ref.at[boxes], ext_o.at[1 + r, inner, mine], local_sem.at[2 + r])
        )
        swaps.append(
            pltpu.make_async_remote_copy(
                src_ref=sketch_ref.at[away],
                dst_ref=ext_o.at[1 + r, inner, mine],
                send_sem=swap_send.at[r],
                recv_sem=swap_recv.at[r],
                device_id=halo.partner,
                device_id_type=MESH,
            )
        )
    for copy in locals_p + locals_o:
        copy.start()
    halo.barrier()
    for copy in swaps:
        copy.start()
    for copy in locals_p:
        copy.wait()
    p_copies = halo.copies(ext_p, p_send, p_recv)
    for copy in p_copies:
        copy.start()

    def own_features(b, carry):
        r, c = 1 + b // TILE, 1 + b % TILE
        value = ext_p[r, c]
        ext_e[r, c] = features(value, False)
        turned[b] = jnp.transpose(features(value, True)).astype(jnp.bfloat16)
        return carry

    lax.fori_loop(0, 8, own_features, 0)
    for copy in locals_o:
        copy.wait()
    for copy in swaps:
        copy.wait_recv()
    o_copies = halo.copies(ext_o, o_send, o_recv)
    for copy in o_copies:
        copy.start()

    def weight_of(b, slot):
        return mask_ref[own * 8 + b, slot].astype(jnp.float32)

    def first_term(b, carry):
        y_ref[b] = ext_o[1 + b // TILE, 1 + b % TILE].astype(jnp.float32) * weight_of(b, 4)
        return carry

    lax.fori_loop(0, 8, first_term, 0)

    def sketch_block(b, slot):
        r, c = b // TILE + slot // 3, b % TILE + slot % 3
        near = (ext_e[r, c] * scale_ref[slot]).astype(jnp.bfloat16)
        weight = weight_of(b, slot)
        step = 128
        for first in range(0, POINTS, step):
            rows = slice(first, first + step)
            square = jnp.dot(turned[b, rows, :], near, preferred_element_type=jnp.float32)
            values = lax.rsqrt(square).astype(jnp.bfloat16)
            kbuf[b, slot, rows, :] = values
            y_ref[b, rows, :] += jnp.dot(values, ext_o[r, c], preferred_element_type=jnp.float32) * weight

    def couple_block(b, slot):
        near = ext_b[b // TILE + slot // 3, b % TILE + slot % 3]
        moved = jnp.dot(kbuf[b, slot], near, preferred_element_type=jnp.float32).astype(jnp.bfloat16)
        value = jnp.dot(basis_t[b], moved, preferred_element_type=jnp.float32)
        stage[b, slot] = value * (weight_of(b, slot) * (1.0 / POINTS))
        keep, give = out_copies(pl.ds(b, 1), pl.ds(slot, 1), own * 8 + b, 1)
        keep.start()
        give.start()

    def out_copies(b, slot, first, count):
        kept = pl.ds(pl.multiple_of(own * rank_half, rank_half), rank_half)
        given = pl.ds(pl.multiple_of(other * rank_half, rank_half), rank_half)
        target = coupling_ref.at[pl.ds(first, count), slot]
        keep = pltpu.make_async_copy(stage.at[b, slot, kept], target, out_sem)
        give = pltpu.make_async_remote_copy(
            src_ref=stage.at[b, slot, given],
            dst_ref=target,
            send_sem=c_send,
            recv_sem=c_recv,
            device_id=halo.partner,
            device_id_type=MESH,
        )
        return keep, give

    def inner_blocks(block):
        def body(t, carry):
            r, q = t // 20, t % 20
            y, p = q // 10 * (1 - 2 * r), q % 10
            some, last = (p + 6) // 10, (p + 3) // 10
            x, c = some - 2 * last, p - 4 * some - 2 * last
            block(r * TILE + c, 3 * (y + 1) + x + 1)
            return carry

        lax.fori_loop(0, 40, body, 0)

    def outer_blocks(block):
        def across(t, carry):
            r, q = t // 12, t % 12
            block(r * TILE + q // 3, 6 * r + q % 3)
            return carry

        lax.fori_loop(0, 24, across, 0)

        def sides(t, carry):
            r, side, y = t // 4, t // 2 % 2, t % 2 * (1 - 2 * (t // 4))
            block(r * TILE + 3 * side, 3 * (y + 1) + 2 * side)
            return carry

        lax.fori_loop(0, 8, sides, 0)

    inner_blocks(sketch_block)
    for copy in p_copies:
        copy.wait_recv()

    def halo_features(t, carry):
        r, c = t // 6, t % 6
        ext_e[3 * r, c] = features(ext_p[3 * r, c], False)
        return carry

    lax.fori_loop(0, 12, halo_features, 0)

    def side_features(t, carry):
        r, c = 1 + t // 2, t % 2 * (TILE + 1)
        ext_e[r, c] = features(ext_p[r, c], False)
        return carry

    lax.fori_loop(0, 4, side_features, 0)
    for copy in o_copies:
        copy.wait_recv()
    outer_blocks(sketch_block)

    def add_units(b, carry):
        same = lax.broadcasted_iota(jnp.int32, (128, 128), 0) == lax.broadcasted_iota(jnp.int32, (128, 128), 1)
        unit = jnp.where(same, 1.0, 0.0)
        for first in range(0, POINTS, 128):
            part = slice(first, first + 128)
            kbuf[b, 4, part, part] = (kbuf[b, 4, part, part].astype(jnp.float32) + unit).astype(jnp.bfloat16)
        return carry

    lax.fori_loop(0, 8, add_units, 0)

    def first_gram(b, carry):
        value = y_ref[b]
        gram = lax.dot_general(value, value, TN, precision=HIGHEST, preferred_element_type=jnp.float32)
        a_ref[b] = gram * (1.0 / POINTS)
        return carry

    def first_apply(b, carry):
        work[b] = lax.dot_general(
            y_ref[b], p_ref[b], NT, precision=HIGHEST, preferred_element_type=jnp.float32
        )
        return carry

    def second_gram(b, carry):
        high, low = parts(work[b], 2)
        cross = lax.dot_general(high, low, TN, preferred_element_type=jnp.float32)
        gram = lax.dot_general(high, high, TN, preferred_element_type=jnp.float32) + (cross + cross.T)
        a_ref[b] = gram * (1.0 / POINTS)
        return carry

    def second_apply(b, carry):
        high, low = parts(work[b], 2)
        p_high, p_low = parts(p_ref[b], 2)
        value = lax.dot_general(high, p_high, NT, preferred_element_type=jnp.float32)
        value += lax.dot_general(high, p_low, NT, preferred_element_type=jnp.float32)
        value += lax.dot_general(low, p_high, NT, preferred_element_type=jnp.float32)
        ext_b[1 + b // TILE, 1 + b % TILE] = value.astype(jnp.bfloat16)
        return carry

    lax.fori_loop(0, 8, first_gram, 0)
    eliminate(a_ref, p_ref, panel_ref)
    lax.fori_loop(0, 8, first_apply, 0)
    lax.fori_loop(0, 8, second_gram, 0)
    eliminate(a_ref, p_ref, panel_ref)
    lax.fori_loop(0, 8, second_apply, 0)

    def turn_basis(b, carry):
        value = ext_b[1 + b // TILE, 1 + b % TILE].astype(jnp.float32)
        basis_t[b] = jnp.transpose(value).astype(jnp.bfloat16)
        return carry

    lax.fori_loop(0, 8, turn_basis, 0)
    b_copies = halo.copies(ext_b, b_send, b_recv)
    for copy in b_copies:
        copy.start()
    keeps, gives = [], []
    for r in range(2):
        boxes = pl.ds(own * 8 + r * TILE, TILE)
        keeps.append(
            pltpu.make_async_copy(ext_b.at[1 + r, inner, mine], basis_ref.at[boxes], local_sem.at[r])
        )
        gives.append(
            pltpu.make_async_remote_copy(
                src_ref=ext_b.at[1 + r, inner, theirs],
                dst_ref=basis_ref.at[boxes],
                send_sem=half_send.at[r],
                recv_sem=half_recv.at[r],
                device_id=halo.partner,
                device_id_type=MESH,
            )
        )
    for copy in keeps + gives:
        copy.start()
    inner_blocks(couple_block)
    for copy in b_copies:
        copy.wait_recv()
    outer_blocks(couple_block)
    keep, give = out_copies(slice(None), slice(None), own * 8, 8)
    keep.wait()
    give.wait()
    for copy in keeps + gives:
        copy.wait()
    for copy in swaps + p_copies + o_copies + b_copies:
        copy.wait_send()


def body(plate, points, sketch, near_mask, scale):
    boxes = points.shape[0]
    mine = boxes // 2
    vmem, hbm, smem = (pl.BlockSpec(memory_space=space) for space in (pltpu.VMEM, pl.ANY, pltpu.SMEM))
    dma = pltpu.SemaphoreType.DMA
    columns = pltpu.VMEM((4, TILE + 2, POINTS, RANK), jnp.bfloat16)
    tall = pltpu.VMEM((mine, POINTS, RANK), jnp.float32)
    square = pltpu.VMEM((mine, RANK, RANK), jnp.float32)
    return pl.pallas_call(
        functools.partial(kernel, plate),
        out_shape=(
            jax.ShapeDtypeStruct((boxes, POINTS // 2, RANK), jnp.bfloat16),
            jax.ShapeDtypeStruct((boxes, SLOTS, RANK // 2, RANK), jnp.float32),
        ),
        in_specs=[smem, hbm, hbm, vmem],
        out_specs=(hbm, hbm),
        scratch_shapes=[
            pltpu.VMEM((4, TILE + 2, 3, POINTS), jnp.bfloat16),
            pltpu.VMEM((4, TILE + 2, FEATURES, POINTS), jnp.float32),
            columns, columns,
            pltpu.VMEM((mine, SLOTS, POINTS, POINTS), jnp.bfloat16),
            pltpu.VMEM((mine, POINTS, FEATURES), jnp.bfloat16),
            tall, tall, square, square,
            pltpu.VMEM((PANEL, mine, RANK), jnp.float32),
            pltpu.VMEM((mine, RANK, POINTS), jnp.bfloat16),
            pltpu.VMEM((mine, SLOTS, RANK, RANK), jnp.float32),
            dma((4,)), dma, dma((2,)), dma((2,)), dma((8,)), dma((8,)), dma((8,)), dma((8,)),
            dma((8,)), dma((8,)), dma((2,)), dma((2,)), dma, dma,
        ],
        compiler_params=pltpu.CompilerParams(collective_id=0, has_side_effects=True, vmem_limit_bytes=LIMIT),
        name="plate_level",
    )(near_mask, points, sketch, scale)


def solution(mesh):
    plate = math.isqrt(mesh.shape["box"])

    def step(points, sketch, near_mask):
        return body(plate, points, sketch, near_mask, jnp.asarray(slot_scales()))

    return jax.shard_map(
        step,
        mesh=mesh,
        in_specs=(P("box", None, None), P("box", "col", None), P("box", None)),
        out_specs=(P("box", "col", None), P("box", None, "col", None)),
        check_vma=False,
    )
```

```python
import functools
import math

import jax
import jax.numpy as jnp
from jax import lax
from jax.experimental import pallas as pl
from jax.experimental.pallas import tpu as pltpu
from jax.sharding import PartitionSpec as P

MESH = pl.DeviceIdType.MESH
HIGHEST = lax.Precision.HIGHEST
TILE = 4
POINTS = 512
RANK = 128
FEATURES = 8
SCALE = math.sqrt(8192.0)
SLOTS = 9
LIMIT = 63 << 20
PANEL = 16
NT = (((1,), (1,)), ((), ()))
TN = (((0,), (0,)), ((), ()))
DIRECTIONS = [(dy, dx) for dy in (-1, 0, 1) for dx in (-1, 0, 1) if (dy, dx) != (0, 0)]


def place(step, side, low, high):
    if step == -1:
        return low
    if step == 1:
        return high
    return slice(1, side + 1)


class Halo:
    def __init__(self, plate):
        self.plate = plate
        box, self.col = lax.axis_index("box"), lax.axis_index("col")
        self.row = box // plate * 2 + self.col
        self.column = box % plate
        self.partner = (box, 1 - self.col)

    def device(self, dy, dx):
        high = self.plate * 2
        row = (self.row + dy + high) % high
        column = (self.column + dx + self.plate) % self.plate
        return (row // 2 * self.plate + column, row % 2)

    def barrier(self):
        sem = pltpu.get_barrier_semaphore()
        for dy, dx in DIRECTIONS:
            pl.semaphore_signal(sem, inc=1, device_id=self.device(dy, dx), device_id_type=MESH)
        pl.semaphore_wait(sem, len(DIRECTIONS))

    def copies(self, ext, send, recv):
        made = []
        for n, (dy, dx) in enumerate(DIRECTIONS):
            made.append(
                pltpu.make_async_remote_copy(
                    src_ref=ext.at[place(dy, 2, 1, 2), place(dx, TILE, 1, TILE)],
                    dst_ref=ext.at[place(dy, 2, 3, 0), place(dx, TILE, TILE + 1, 0)],
                    send_sem=send.at[n],
                    recv_sem=recv.at[n],
                    device_id=self.device(dy, dx),
                    device_id_type=MESH,
                )
            )
        return made


def parts(value, count):
    made = []
    for _ in range(count):
        made.append(value.astype(jnp.bfloat16))
        value = value - made[-1].astype(jnp.float32)
    return made


def features(points):
    wide = points.astype(jnp.float32)
    u, v = (wide[0:1] - 0.5) * SCALE, (wide[1:2] - 0.5) * SCALE
    h = (wide[2:3] - 0.5) * (0.25 * SCALE)
    at = lax.broadcasted_iota(jnp.int32, (FEATURES, POINTS), 0)
    rest = jnp.where(at == 2, h, u * u + v * v + h * h)
    return jnp.where(at == 0, u, jnp.where(at == 1, v, rest))


def eliminate(a_ref, p_ref, panel_ref):
    boxes, rank = a_ref.shape[0], a_ref.shape[1]
    lane = lax.broadcasted_iota(jnp.int32, (boxes, rank), 1)
    row_id = lax.broadcasted_iota(jnp.int32, (rank, rank), 0)
    col_id = lax.broadcasted_iota(jnp.int32, (rank, rank), 1)

    def panel(n, carry):
        first = pl.multiple_of(n * PANEL, PANEL)
        for b in range(boxes):
            panel_ref[:, b, :] = a_ref[b, pl.ds(first, PANEL), :]
        rows = [panel_ref[i] for i in range(PANEL)]
        for k in range(PANEL):
            here = lane == first + k
            index = jnp.full((boxes, rank), first + k, jnp.int32)
            pivot = jnp.take_along_axis(rows[k], index, axis=1)
            inverse = 1.0 / pivot
            scaled = jnp.where(here, inverse, rows[k] * inverse)
            for i in range(k + 1, PANEL):
                factor = jnp.take_along_axis(rows[i], index, axis=1)
                rows[i] = jnp.where(here, 0.0, rows[i]) - factor * scaled
            keep = (lane < first + k) | (lane >= first + PANEL)
            rows[k] = jnp.where(keep, rows[k], jnp.where(here, 1.0, 0.0)) * lax.rsqrt(pivot)
        for i in range(PANEL):
            panel_ref[i] = rows[i]
        below = row_id >= first + PANEL
        inside = (col_id >= first) & (col_id < first + PANEL)
        for b in range(boxes):
            own = panel_ref[:, b, :]
            p_ref[b, pl.ds(first, PANEL), :] = jnp.where(col_id[:PANEL] <= row_id[:PANEL] + first, own, 0.0)
            w1, w2, w3 = parts(own, 3)
            left = jnp.concatenate([w1, w1, w2, w1, w2, w3], 0)
            right = jnp.concatenate([w1, w2, w1, w3, w2, w1], 0)
            update = lax.dot_general(left, right, TN, preferred_element_type=jnp.float32)
            old = a_ref[b]
            a_ref[b] = jnp.where(below, jnp.where(inside, 0.0, old) - update, old)
        return carry

    lax.fori_loop(0, rank // PANEL, panel, 0)


def block_of(t):
    rest, side = t // 40, t // 64
    r, q = t // 20, t % 20
    y, p = q // 10 * (1 - 2 * r), q % 10
    some, last = (p + 6) // 10, (p + 3) // 10
    inner_b = r * TILE + p - 4 * some - 2 * last
    inner_slot = 3 * (y + 1) + some - 2 * last + 1
    n = t - 40
    r, q = n // 12, n % 12
    across_b, across_slot = r * TILE + q // 3, 6 * r + q % 3
    n = t - 64
    r, right, y = n // 4, n // 2 % 2, n % 2 * (1 - 2 * (n // 4))
    side_b, side_slot = r * TILE + 3 * right, 3 * (y + 1) + 2 * right
    b = inner_b * (1 - rest) + across_b * (rest - side) + side_b * side
    slot = inner_slot * (1 - rest) + across_slot * (rest - side) + side_slot * side
    return b, slot


def pair_of(u):
    below, down, back = (u + 10) // 16, (u + 6) // 16, (u + 3) // 16
    r = u // 3 * (1 - below)
    c = u % 3 * (1 - below) + (u - 6) * (below - down) + (u - 10) * (down - back) + (u - 12) * back
    x = 1 - below + down - 2 * back
    return r * TILE + c, 3 * (below + 1) + x + 1


def kernel(
    plate, mask_ref, points_ref, sketch_ref, basis_ref, coupling_ref,
    ext_p, ext_e, ext_o, ext_b, kbuf, even, odd, turned, y_ref, work, a_ref, p_ref, panel_ref, basis_t, stage,
    local_sem, out_sem, swap_send, swap_recv, p_send, p_recv, o_send, o_recv,
    b_send, b_recv, half_send, half_recv, c_send, c_recv,
):
    halo = Halo(plate)
    own, other = halo.col, 1 - halo.col
    half = sketch_ref.shape[1]
    rank_half = coupling_ref.shape[2]
    inner = slice(1, TILE + 1)
    mine = pl.ds(pl.multiple_of(own * half, half), half)
    theirs = pl.ds(pl.multiple_of(other * half, half), half)
    locals_p, locals_o, swaps = [], [], []
    for r in range(2):
        boxes = pl.ds(own * 8 + r * TILE, TILE)
        away = pl.ds(other * 8 + r * TILE, TILE)
        locals_p.append(pltpu.make_async_copy(points_ref.at[boxes], ext_p.at[1 + r, inner], local_sem.at[r]))
        locals_o.append(
            pltpu.make_async_copy(sketch_ref.at[boxes], ext_o.at[1 + r, inner, mine], local_sem.at[2 + r])
        )
        swaps.append(
            pltpu.make_async_remote_copy(
                src_ref=sketch_ref.at[away],
                dst_ref=ext_o.at[1 + r, inner, mine],
                send_sem=swap_send.at[r],
                recv_sem=swap_recv.at[r],
                device_id=halo.partner,
                device_id_type=MESH,
            )
        )
    for copy in locals_p + locals_o:
        copy.start()
    halo.barrier()
    for copy in swaps:
        copy.start()
    for copy in locals_p:
        copy.wait()
    p_copies = halo.copies(ext_p, p_send, p_recv)
    for copy in p_copies:
        copy.start()

    def own_features(b, carry):
        r, c = 1 + b // TILE, 1 + b % TILE
        value = features(ext_p[r, c])
        ext_e[r, c] = value
        turned[b] = jnp.transpose(value)
        return carry

    lax.fori_loop(0, 8, own_features, 0)
    for copy in locals_o:
        copy.wait()
    for copy in swaps:
        copy.wait_recv()
    o_copies = halo.copies(ext_o, o_send, o_recv)
    for copy in o_copies:
        copy.start()

    def weight_of(b, slot):
        return mask_ref[own * 8 + b, slot].astype(jnp.float32)

    def first_term(b, carry):
        y_ref[b] = ext_o[1 + b // TILE, 1 + b % TILE].astype(jnp.float32) * weight_of(b, 4)
        return carry

    lax.fori_loop(0, 8, first_term, 0)

    def fill_block(t, copy_ref):
        b, slot = block_of(t)
        near = ext_e[b // TILE + slot // 3, b % TILE + slot % 3]
        u = near[0:1] + (slot % 3 - 1) * SCALE
        v = near[1:2] + (slot // 3 - 1) * SCALE
        h = near[2:3]
        norm = u * u + v * v + h * h + 4.0
        u, v, h = -2.0 * u, -2.0 * v, -2.0 * h
        step = 64
        for first in range(0, POINTS, step):
            rows = slice(first, first + step)
            own_rows = turned[b, rows, :]
            square = (own_rows[:, 3:4] + norm) + own_rows[:, 0:1] * u
            square = square + (own_rows[:, 1:2] * v + own_rows[:, 2:3] * h)
            values = lax.rsqrt(square).astype(jnp.bfloat16)
            kbuf[b, slot, rows, :] = values
            copy_ref[rows, :] = values

    def add_block(t, copy_ref):
        b, slot = block_of(t)
        near = ext_o[b // TILE + slot // 3, b % TILE + slot % 3]
        y_ref[b] += jnp.dot(copy_ref[...], near, preferred_element_type=jnp.float32) * weight_of(b, slot)

    def sketch_pair(i, carry):
        t = 2 * i
        add_block(t, even)
        fill_block(t + 1, odd)
        add_block(t + 1, odd)
        fill_block(jnp.minimum(t + 2, 71), even)
        return carry

    def couple_blocks(blocks, mirrored):
        moved = []
        for b, slot in blocks:
            value = jnp.dot(basis_t[b], kbuf[b, slot], preferred_element_type=jnp.float32)
            moved.append(value.astype(jnp.bfloat16))
        for (b, slot), value in zip(blocks, moved):
            y, x = slot // 3 - 1, slot % 3 - 1
            near = ext_b[b // TILE + 1 + y, b % TILE + 1 + x]
            value = jnp.dot(value, near, preferred_element_type=jnp.float32) * (1.0 / POINTS)
            stage[b, slot] = value * weight_of(b, slot)
            start_out(b, slot)
            if mirrored:
                other_b = b + TILE * y + x
                stage[other_b, 8 - slot] = value.T * weight_of(other_b, 8 - slot)
                start_out(other_b, 8 - slot)

    def start_out(b, slot):
        keep, give = out_copies(pl.ds(b, 1), pl.ds(slot, 1), own * 8 + b, 1)
        keep.start()
        give.start()

    def out_copies(b, slot, first, count):
        kept = pl.ds(pl.multiple_of(own * rank_half, rank_half), rank_half)
        given = pl.ds(pl.multiple_of(other * rank_half, rank_half), rank_half)
        target = coupling_ref.at[pl.ds(first, count), slot]
        keep = pltpu.make_async_copy(stage.at[b, slot, kept], target, out_sem)
        give = pltpu.make_async_remote_copy(
            src_ref=stage.at[b, slot, given],
            dst_ref=target,
            send_sem=c_send,
            recv_sem=c_recv,
            device_id=halo.partner,
            device_id_type=MESH,
        )
        return keep, give

    fill_block(0, even)
    lax.fori_loop(0, 19, sketch_pair, 0)
    for copy in p_copies:
        copy.wait_recv()

    def halo_features(t, carry):
        r, c = t // 6, t % 6
        ext_e[3 * r, c] = features(ext_p[3 * r, c])
        return carry

    lax.fori_loop(0, 12, halo_features, 0)

    def side_features(t, carry):
        r, c = 1 + t // 2, t % 2 * (TILE + 1)
        ext_e[r, c] = features(ext_p[r, c])
        return carry

    lax.fori_loop(0, 4, side_features, 0)
    for copy in o_copies:
        copy.wait_recv()
    lax.fori_loop(19, 36, sketch_pair, 0)

    def add_units(b, carry):
        same = lax.broadcasted_iota(jnp.int32, (128, 128), 0) == lax.broadcasted_iota(jnp.int32, (128, 128), 1)
        unit = jnp.where(same, 1.0, 0.0)
        for first in range(0, POINTS, 128):
            part = slice(first, first + 128)
            kbuf[b, 4, part, part] = (kbuf[b, 4, part, part].astype(jnp.float32) + unit).astype(jnp.bfloat16)
        return carry

    lax.fori_loop(0, 8, add_units, 0)

    def first_gram(b, carry):
        value = y_ref[b]
        gram = lax.dot_general(value, value, TN, precision=HIGHEST, preferred_element_type=jnp.float32)
        a_ref[b] = gram * (1.0 / POINTS)
        return carry

    def first_apply(b, carry):
        work[b] = lax.dot_general(
            y_ref[b], p_ref[b], NT, precision=HIGHEST, preferred_element_type=jnp.float32
        )
        return carry

    def second_gram(b, carry):
        high, low = parts(work[b], 2)
        cross = lax.dot_general(high, low, TN, preferred_element_type=jnp.float32)
        gram = lax.dot_general(high, high, TN, preferred_element_type=jnp.float32) + (cross + cross.T)
        a_ref[b] = gram * (1.0 / POINTS)
        return carry

    def second_apply(b, carry):
        high, low = parts(work[b], 2)
        p_high, p_low = parts(p_ref[b], 2)
        value = lax.dot_general(high, p_high, NT, preferred_element_type=jnp.float32)
        value += lax.dot_general(high, p_low, NT, preferred_element_type=jnp.float32)
        value += lax.dot_general(low, p_high, NT, preferred_element_type=jnp.float32)
        ext_b[1 + b // TILE, 1 + b % TILE] = value.astype(jnp.bfloat16)
        return carry

    lax.fori_loop(0, 8, first_gram, 0)
    eliminate(a_ref, p_ref, panel_ref)
    lax.fori_loop(0, 8, first_apply, 0)
    lax.fori_loop(0, 8, second_gram, 0)
    eliminate(a_ref, p_ref, panel_ref)
    lax.fori_loop(0, 8, second_apply, 0)

    def turn_basis(b, carry):
        value = ext_b[1 + b // TILE, 1 + b % TILE].astype(jnp.float32)
        basis_t[b] = jnp.transpose(value).astype(jnp.bfloat16)
        return carry

    lax.fori_loop(0, 8, turn_basis, 0)
    b_copies = halo.copies(ext_b, b_send, b_recv)
    for copy in b_copies:
        copy.start()
    keeps, gives = [], []
    for r in range(2):
        boxes = pl.ds(own * 8 + r * TILE, TILE)
        keeps.append(
            pltpu.make_async_copy(ext_b.at[1 + r, inner, mine], basis_ref.at[boxes], local_sem.at[r])
        )
        gives.append(
            pltpu.make_async_remote_copy(
                src_ref=ext_b.at[1 + r, inner, theirs],
                dst_ref=basis_ref.at[boxes],
                send_sem=half_send.at[r],
                recv_sem=half_recv.at[r],
                device_id=halo.partner,
                device_id_type=MESH,
            )
        )
    for copy in keeps + gives:
        copy.start()

    def couple_centres(i, carry):
        couple_blocks([(2 * i, 4), (2 * i + 1, 4)], False)
        return carry

    def couple_pairs(i, carry):
        couple_blocks([pair_of(2 * i), pair_of(2 * i + 1)], True)
        return carry

    def couple_rest(i, carry):
        couple_blocks([block_of(2 * i), block_of(2 * i + 1)], False)
        return carry

    lax.fori_loop(0, 4, couple_centres, 0)
    lax.fori_loop(0, 8, couple_pairs, 0)
    for copy in b_copies:
        copy.wait_recv()
    lax.fori_loop(20, 36, couple_rest, 0)
    keep, give = out_copies(slice(None), slice(None), own * 8, 8)
    keep.wait()
    give.wait()
    for copy in keeps + gives:
        copy.wait()
    for copy in swaps + p_copies + o_copies + b_copies:
        copy.wait_send()


def body(plate, points, sketch, near_mask):
    boxes = points.shape[0]
    mine = boxes // 2
    hbm, smem = (pl.BlockSpec(memory_space=space) for space in (pl.ANY, pltpu.SMEM))
    dma = pltpu.SemaphoreType.DMA
    columns = pltpu.VMEM((4, TILE + 2, POINTS, RANK), jnp.bfloat16)
    tall = pltpu.VMEM((mine, POINTS, RANK), jnp.float32)
    square = pltpu.VMEM((mine, RANK, RANK), jnp.float32)
    return pl.pallas_call(
        functools.partial(kernel, plate),
        out_shape=(
            jax.ShapeDtypeStruct((boxes, POINTS // 2, RANK), jnp.bfloat16),
            jax.ShapeDtypeStruct((boxes, SLOTS, RANK // 2, RANK), jnp.float32),
        ),
        in_specs=[smem, hbm, hbm],
        out_specs=(hbm, hbm),
        scratch_shapes=[
            pltpu.VMEM((4, TILE + 2, 3, POINTS), jnp.bfloat16),
            pltpu.VMEM((4, TILE + 2, FEATURES, POINTS), jnp.float32),
            columns, columns,
            pltpu.VMEM((mine, SLOTS, POINTS, POINTS), jnp.bfloat16),
            pltpu.VMEM((POINTS, POINTS), jnp.bfloat16),
            pltpu.VMEM((POINTS, POINTS), jnp.bfloat16),
            pltpu.VMEM((mine, POINTS, FEATURES), jnp.float32),
            tall, tall, square, square,
            pltpu.VMEM((PANEL, mine, RANK), jnp.float32),
            pltpu.VMEM((mine, RANK, POINTS), jnp.bfloat16),
            pltpu.VMEM((mine, SLOTS, RANK, RANK), jnp.float32),
            dma((4,)), dma, dma((2,)), dma((2,)), dma((8,)), dma((8,)), dma((8,)), dma((8,)),
            dma((8,)), dma((8,)), dma((2,)), dma((2,)), dma, dma,
        ],
        compiler_params=pltpu.CompilerParams(collective_id=0, has_side_effects=True, vmem_limit_bytes=LIMIT),
        name="plate_level",
    )(near_mask, points, sketch)


def solution(mesh):
    plate = math.isqrt(mesh.shape["box"])

    def step(points, sketch, near_mask):
        return body(plate, points, sketch, near_mask)

    return jax.shard_map(
        step,
        mesh=mesh,
        in_specs=(P("box", None, None), P("box", "col", None), P("box", None)),
        out_specs=(P("box", "col", None), P("box", None, "col", None)),
        check_vma=False,
    )
```

```python
import functools
import math

import jax
import jax.numpy as jnp
from jax import lax
from jax.experimental import pallas as pl
from jax.experimental.pallas import tpu as pltpu
from jax.sharding import PartitionSpec as P

MESH = pl.DeviceIdType.MESH
HIGHEST = lax.Precision.HIGHEST
TILE = 4
POINTS = 512
RANK = 128
FEATURES = 8
SCALE = math.sqrt(8192.0)
SLOTS = 9
LIMIT = 63 << 20
PANEL = 16
NT = (((1,), (1,)), ((), ()))
TN = (((0,), (0,)), ((), ()))
DIRECTIONS = [(dy, dx) for dy in (-1, 0, 1) for dx in (-1, 0, 1) if (dy, dx) != (0, 0)]


def place(step, side, low, high):
    if step == -1:
        return low
    if step == 1:
        return high
    return slice(1, side + 1)


class Halo:
    def __init__(self, plate):
        self.plate = plate
        box, self.col = lax.axis_index("box"), lax.axis_index("col")
        self.row = box // plate * 2 + self.col
        self.column = box % plate
        self.partner = (box, 1 - self.col)

    def device(self, dy, dx):
        high = self.plate * 2
        row = (self.row + dy + high) % high
        column = (self.column + dx + self.plate) % self.plate
        return (row // 2 * self.plate + column, row % 2)

    def barrier(self):
        sem = pltpu.get_barrier_semaphore()
        for dy, dx in DIRECTIONS:
            pl.semaphore_signal(sem, inc=1, device_id=self.device(dy, dx), device_id_type=MESH)
        pl.semaphore_wait(sem, len(DIRECTIONS))

    def copies(self, own, at, ext, send, recv):
        made = []
        for n, (dy, dx) in enumerate(DIRECTIONS):
            rows = (slice(at, at + 2), at, at + 1)
            columns = (slice(at, at + TILE), at, at + TILE - 1)
            made.append(
                pltpu.make_async_remote_copy(
                    src_ref=own.at[rows[0 if dy == 0 else (3 + dy) // 2], columns[0 if dx == 0 else (3 + dx) // 2]],
                    dst_ref=ext.at[place(dy, 2, 3, 0), place(dx, TILE, TILE + 1, 0)],
                    send_sem=send.at[n],
                    recv_sem=recv.at[n],
                    device_id=self.device(dy, dx),
                    device_id_type=MESH,
                )
            )
        return made


def parts(value, count):
    made = []
    for _ in range(count):
        made.append(value.astype(jnp.bfloat16))
        value = value - made[-1].astype(jnp.float32)
    return made


def features(points):
    wide = points.astype(jnp.float32)
    u, v = (wide[0:1] - 0.5) * SCALE, (wide[1:2] - 0.5) * SCALE
    h = (wide[2:3] - 0.5) * (0.25 * SCALE)
    at = lax.broadcasted_iota(jnp.int32, (FEATURES, POINTS), 0)
    rest = jnp.where(at == 2, h, u * u + v * v + h * h)
    return jnp.where(at == 0, u, jnp.where(at == 1, v, rest))


def eliminate(a_ref, p_ref, panel_ref):
    boxes, rank = a_ref.shape[0], a_ref.shape[1]
    lane = lax.broadcasted_iota(jnp.int32, (boxes, rank), 1)
    row_id = lax.broadcasted_iota(jnp.int32, (rank, rank), 0)
    col_id = lax.broadcasted_iota(jnp.int32, (rank, rank), 1)

    def panel(n, carry):
        first = pl.multiple_of(n * PANEL, PANEL)
        for b in range(boxes):
            panel_ref[:, b, :] = a_ref[b, pl.ds(first, PANEL), :]
        rows = [panel_ref[i] for i in range(PANEL)]
        for k in range(0, PANEL, 2):
            here, there = lane == first + k, lane == first + k + 1
            both = here | there
            index = jnp.full((boxes, rank), first + k, jnp.int32)
            upper, lower = rows[k], rows[k + 1]
            p = jnp.take_along_axis(upper, index, axis=1)
            q = jnp.take_along_axis(lower, index, axis=1)
            s = jnp.take_along_axis(lower, index + 1, axis=1)
            det = p * s - q * q
            ratio = 1.0 / p
            last = (1.0 / det) * p
            share = q * ratio
            upper = jnp.where(both, jnp.where(here, 1.0, 0.0), upper)
            lower = jnp.where(both, jnp.where(there, 1.0, 0.0), lower) - share * upper
            x, y = upper * ratio, lower * last
            for i in range(k + 2, PANEL):
                f = jnp.take_along_axis(rows[i], index, axis=1)
                g = jnp.take_along_axis(rows[i], index + 1, axis=1) - f * share
                rows[i] = (jnp.where(both, 0.0, rows[i]) - f * x) - g * y
            outside = (lane < first) | (lane >= first + PANEL)
            rows[k] = jnp.where(outside | (lane <= first + k), upper, 0.0) * lax.rsqrt(p)
            rows[k + 1] = jnp.where(outside | (lane <= first + k + 1), lower, 0.0) * lax.sqrt(last)
        for i in range(PANEL):
            panel_ref[i] = rows[i]
        below = row_id >= first + PANEL
        inside = (col_id >= first) & (col_id < first + PANEL)
        for b in range(boxes):
            own = panel_ref[:, b, :]
            p_ref[b, pl.ds(first, PANEL), :] = jnp.where(col_id[:PANEL] <= row_id[:PANEL] + first, own, 0.0)
            w1, w2, w3 = parts(own, 3)
            left = jnp.concatenate([w1, w1, w2, w1, w2, w3], 0)
            right = jnp.concatenate([w1, w2, w1, w3, w2, w1], 0)
            update = lax.dot_general(left, right, TN, preferred_element_type=jnp.float32)
            old = a_ref[b]
            a_ref[b] = jnp.where(below, jnp.where(inside, 0.0, old) - update, old)
        return carry

    lax.fori_loop(0, rank // PANEL, panel, 0)


def block_of(t):
    rest, side = t // 40, t // 64
    r, q = t // 20, t % 20
    y, p = q // 10 * (1 - 2 * r), q % 10
    some, last = (p + 6) // 10, (p + 3) // 10
    inner_b = r * TILE + p - 4 * some - 2 * last
    inner_slot = 3 * (y + 1) + some - 2 * last + 1
    n = t - 40
    r, q = n // 12, n % 12
    across_b, across_slot = r * TILE + q // 3, 6 * r + q % 3
    n = t - 64
    r, right, y = n // 4, n // 2 % 2, n % 2 * (1 - 2 * (n // 4))
    side_b, side_slot = r * TILE + 3 * right, 3 * (y + 1) + 2 * right
    b = inner_b * (1 - rest) + across_b * (rest - side) + side_b * side
    slot = inner_slot * (1 - rest) + across_slot * (rest - side) + side_slot * side
    return b, slot


def pair_of(u):
    below, down, back = (u + 10) // 16, (u + 6) // 16, (u + 3) // 16
    r = u // 3 * (1 - below)
    c = u % 3 * (1 - below) + (u - 6) * (below - down) + (u - 10) * (down - back) + (u - 12) * back
    x = 1 - below + down - 2 * back
    return r * TILE + c, 3 * (below + 1) + x + 1


def kernel(
    plate, mask_ref, points_ref, sketch_ref, basis_ref, coupling_ref,
    ext_p, ext_e, ext_o, ext_b, ext_d, rough, kbuf, even, odd, turned, y_ref, work, a_ref, p_ref, panel_ref, scale_ref, basis_t, stage,
    local_sem, out_sem, swap_send, swap_recv, p_send, p_recv, o_send, o_recv,
    b_send, b_recv, d_send, d_recv, half_send, half_recv, c_send, c_recv,
):
    halo = Halo(plate)
    own, other = halo.col, 1 - halo.col
    half = sketch_ref.shape[1]
    rank_half = coupling_ref.shape[2]
    inner = slice(1, TILE + 1)
    mine = pl.ds(pl.multiple_of(own * half, half), half)
    theirs = pl.ds(pl.multiple_of(other * half, half), half)
    locals_p, locals_o, swaps = [], [], []
    for r in range(2):
        boxes = pl.ds(own * 8 + r * TILE, TILE)
        away = pl.ds(other * 8 + r * TILE, TILE)
        locals_p.append(pltpu.make_async_copy(points_ref.at[boxes], ext_p.at[1 + r, inner], local_sem.at[r]))
        locals_o.append(
            pltpu.make_async_copy(sketch_ref.at[boxes], ext_o.at[1 + r, inner, mine], local_sem.at[2 + r])
        )
        swaps.append(
            pltpu.make_async_remote_copy(
                src_ref=sketch_ref.at[away],
                dst_ref=ext_o.at[1 + r, inner, mine],
                send_sem=swap_send.at[r],
                recv_sem=swap_recv.at[r],
                device_id=halo.partner,
                device_id_type=MESH,
            )
        )
    for copy in locals_p + locals_o:
        copy.start()
    halo.barrier()
    for copy in swaps:
        copy.start()
    for copy in locals_p:
        copy.wait()
    p_copies = halo.copies(ext_p, 1, ext_p, p_send, p_recv)
    for copy in p_copies:
        copy.start()

    def own_features(b, carry):
        r, c = 1 + b // TILE, 1 + b % TILE
        value = features(ext_p[r, c])
        ext_e[r, c] = value
        turned[b] = jnp.transpose(value)
        return carry

    lax.fori_loop(0, 8, own_features, 0)
    for copy in locals_o:
        copy.wait()
    for copy in swaps:
        copy.wait_recv()
    o_copies = halo.copies(ext_o, 1, ext_o, o_send, o_recv)
    for copy in o_copies:
        copy.start()

    def weight_of(b, slot):
        return mask_ref[own * 8 + b, slot].astype(jnp.float32)

    def first_term(b, carry):
        y_ref[b] = ext_o[1 + b // TILE, 1 + b % TILE].astype(jnp.float32) * weight_of(b, 4)
        return carry

    lax.fori_loop(0, 8, first_term, 0)

    def fill_block(t, copy_ref):
        b, slot = block_of(t)
        near = ext_e[b // TILE + slot // 3, b % TILE + slot % 3]
        u = near[0:1] + (slot % 3 - 1) * SCALE
        v = near[1:2] + (slot // 3 - 1) * SCALE
        h = near[2:3]
        norm = u * u + v * v + h * h + 4.0
        u, v, h = -2.0 * u, -2.0 * v, -2.0 * h
        step = 64
        for first in range(0, POINTS, step):
            rows = slice(first, first + step)
            own_rows = turned[b, rows, :]
            square = (own_rows[:, 3:4] + norm) + own_rows[:, 0:1] * u
            square = square + (own_rows[:, 1:2] * v + own_rows[:, 2:3] * h)
            values = lax.rsqrt(square).astype(jnp.bfloat16)
            kbuf[b, slot, rows, :] = values
            copy_ref[rows, :] = values

    def add_block(t, copy_ref):
        b, slot = block_of(t)
        near = ext_o[b // TILE + slot // 3, b % TILE + slot % 3]
        y_ref[b] += jnp.dot(copy_ref[...], near, preferred_element_type=jnp.float32) * weight_of(b, slot)

    def sketch_pair(i, carry):
        t = 2 * i
        add_block(t, even)
        fill_block(t + 1, odd)
        add_block(t + 1, odd)
        fill_block(jnp.minimum(t + 2, 71), even)
        return carry

    def couple_blocks(blocks, mirrored):
        moved = []
        for b, slot in blocks:
            value = jnp.dot(basis_t[b], kbuf[b, slot], preferred_element_type=jnp.float32)
            moved.append(value.astype(jnp.bfloat16))
        for (b, slot), value in zip(blocks, moved):
            y, x = slot // 3 - 1, slot % 3 - 1
            near = ext_b[b // TILE + 1 + y, b % TILE + 1 + x]
            value = jnp.dot(value, near, preferred_element_type=jnp.float32) * (1.0 / POINTS)
            stage[b, slot] = value * weight_of(b, slot)
            start_out(b, slot)
            if mirrored:
                other_b = b + TILE * y + x
                stage[other_b, 8 - slot] = value.T * weight_of(other_b, 8 - slot)
                start_out(other_b, 8 - slot)

    def start_out(b, slot):
        keep, give = out_copies(pl.ds(b, 1), pl.ds(slot, 1), own * 8 + b, 1)
        keep.start()
        give.start()

    def out_copies(b, slot, first, count):
        kept = pl.ds(pl.multiple_of(own * rank_half, rank_half), rank_half)
        given = pl.ds(pl.multiple_of(other * rank_half, rank_half), rank_half)
        target = coupling_ref.at[pl.ds(first, count), slot]
        keep = pltpu.make_async_copy(stage.at[b, slot, kept], target, out_sem)
        give = pltpu.make_async_remote_copy(
            src_ref=stage.at[b, slot, given],
            dst_ref=target,
            send_sem=c_send,
            recv_sem=c_recv,
            device_id=halo.partner,
            device_id_type=MESH,
        )
        return keep, give

    fill_block(0, even)
    lax.fori_loop(0, 19, sketch_pair, 0)
    for copy in p_copies:
        copy.wait_recv()

    def halo_features(t, carry):
        r, c = t // 6, t % 6
        ext_e[3 * r, c] = features(ext_p[3 * r, c])
        return carry

    lax.fori_loop(0, 12, halo_features, 0)

    def side_features(t, carry):
        r, c = 1 + t // 2, t % 2 * (TILE + 1)
        ext_e[r, c] = features(ext_p[r, c])
        return carry

    lax.fori_loop(0, 4, side_features, 0)
    for copy in o_copies:
        copy.wait_recv()
    lax.fori_loop(19, 36, sketch_pair, 0)

    def add_units(b, carry):
        same = lax.broadcasted_iota(jnp.int32, (128, 128), 0) == lax.broadcasted_iota(jnp.int32, (128, 128), 1)
        unit = jnp.where(same, 1.0, 0.0)
        for first in range(0, POINTS, 128):
            part = slice(first, first + 128)
            kbuf[b, 4, part, part] = (kbuf[b, 4, part, part].astype(jnp.float32) + unit).astype(jnp.bfloat16)
        return carry

    lax.fori_loop(0, 8, add_units, 0)

    def first_gram(b, carry):
        value = y_ref[b]
        gram = lax.dot_general(value, value, TN, precision=HIGHEST, preferred_element_type=jnp.float32)
        at = [lax.broadcasted_iota(jnp.int32, (RANK, RANK), axis) for axis in (0, 1)]
        diagonal = jnp.where(at[0] == at[1], gram, 0.0)
        along, across = [lax.rsqrt(jnp.sum(diagonal, axis=axis, keepdims=True)) for axis in (0, 1)]
        a_ref[b] = gram * along * across
        scale_ref[b] = jnp.broadcast_to(along * math.sqrt(POINTS), (8, RANK))
        return carry

    def first_apply(b, carry):
        value = lax.dot_general(
            y_ref[b], p_ref[b] * scale_ref[b, 0:1], NT, precision=HIGHEST, preferred_element_type=jnp.float32
        )
        work[b] = value
        rough[b // TILE, b % TILE] = value.astype(jnp.bfloat16)
        return carry

    def second_gram(b, carry):
        high, low = parts(work[b], 2)
        cross = lax.dot_general(high, low, TN, preferred_element_type=jnp.float32)
        gram = lax.dot_general(high, high, TN, preferred_element_type=jnp.float32) + (cross + cross.T)
        a_ref[b] = gram * (1.0 / POINTS)
        return carry

    def second_apply(b, carry):
        high, low = parts(work[b], 2)
        p_high, p_low = parts(p_ref[b], 2)
        value = lax.dot_general(high, p_high, NT, preferred_element_type=jnp.float32)
        value += lax.dot_general(high, p_low, NT, preferred_element_type=jnp.float32)
        value += lax.dot_general(low, p_high, NT, preferred_element_type=jnp.float32)
        ext_b[1 + b // TILE, 1 + b % TILE] = value.astype(jnp.bfloat16)
        return carry

    lax.fori_loop(0, 8, first_gram, 0)
    eliminate(a_ref, p_ref, panel_ref)
    lax.fori_loop(0, 8, first_apply, 0)
    lax.fori_loop(0, 8, second_gram, 0)
    b_copies = halo.copies(rough, 0, ext_b, b_send, b_recv)
    for copy in b_copies:
        copy.start()
    eliminate(a_ref, p_ref, panel_ref)

    def step_of(b, carry):
        at = [lax.broadcasted_iota(jnp.int32, (RANK, RANK), axis) for axis in (0, 1)]
        step = p_ref[b] - jnp.where(at[0] == at[1], 1.0, 0.0)
        ext_d[1 + b // TILE, 1 + b % TILE] = step.astype(jnp.bfloat16)
        return carry

    lax.fori_loop(0, 8, step_of, 0)
    lax.fori_loop(0, 8, second_apply, 0)
    d_copies = halo.copies(ext_d, 1, ext_d, d_send, d_recv)
    for copy in d_copies:
        copy.start()

    def turn_basis(b, carry):
        value = ext_b[1 + b // TILE, 1 + b % TILE].astype(jnp.float32)
        basis_t[b] = jnp.transpose(value).astype(jnp.bfloat16)
        return carry

    lax.fori_loop(0, 8, turn_basis, 0)
    keeps, gives = [], []
    for r in range(2):
        boxes = pl.ds(own * 8 + r * TILE, TILE)
        keeps.append(
            pltpu.make_async_copy(ext_b.at[1 + r, inner, mine], basis_ref.at[boxes], local_sem.at[r])
        )
        gives.append(
            pltpu.make_async_remote_copy(
                src_ref=ext_b.at[1 + r, inner, theirs],
                dst_ref=basis_ref.at[boxes],
                send_sem=half_send.at[r],
                recv_sem=half_recv.at[r],
                device_id=halo.partner,
                device_id_type=MESH,
            )
        )
    for copy in keeps + gives:
        copy.start()

    def couple_centres(i, carry):
        couple_blocks([(2 * i, 4), (2 * i + 1, 4)], False)
        return carry

    def couple_pairs(i, carry):
        couple_blocks([pair_of(2 * i), pair_of(2 * i + 1)], True)
        return carry

    def couple_rest(i, carry):
        couple_blocks([block_of(2 * i), block_of(2 * i + 1)], False)
        return carry

    lax.fori_loop(0, 4, couple_centres, 0)
    lax.fori_loop(0, 8, couple_pairs, 0)
    for copy in b_copies + d_copies:
        copy.wait_recv()

    def finish_near(r, c):
        near = ext_b[r, c]
        change = lax.dot_general(near, ext_d[r, c], NT, preferred_element_type=jnp.float32)
        ext_b[r, c] = (near.astype(jnp.float32) + change).astype(jnp.bfloat16)

    def finish_across(t, carry):
        finish_near(3 * (t // 6), t % 6)
        return carry

    def finish_side(t, carry):
        finish_near(1 + t // 2, t % 2 * (TILE + 1))
        return carry

    lax.fori_loop(0, 12, finish_across, 0)
    lax.fori_loop(0, 4, finish_side, 0)
    lax.fori_loop(20, 36, couple_rest, 0)
    keep, give = out_copies(slice(None), slice(None), own * 8, 8)
    keep.wait()
    give.wait()
    for copy in keeps + gives:
        copy.wait()
    for copy in swaps + p_copies + o_copies + b_copies + d_copies:
        copy.wait_send()


def body(plate, points, sketch, near_mask):
    boxes = points.shape[0]
    mine = boxes // 2
    hbm, smem = (pl.BlockSpec(memory_space=space) for space in (pl.ANY, pltpu.SMEM))
    dma = pltpu.SemaphoreType.DMA
    columns = pltpu.VMEM((4, TILE + 2, POINTS, RANK), jnp.bfloat16)
    tall = pltpu.VMEM((mine, POINTS, RANK), jnp.float32)
    square = pltpu.VMEM((mine, RANK, RANK), jnp.float32)
    return pl.pallas_call(
        functools.partial(kernel, plate),
        out_shape=(
            jax.ShapeDtypeStruct((boxes, POINTS // 2, RANK), jnp.bfloat16),
            jax.ShapeDtypeStruct((boxes, SLOTS, RANK // 2, RANK), jnp.float32),
        ),
        in_specs=[smem, hbm, hbm],
        out_specs=(hbm, hbm),
        scratch_shapes=[
            pltpu.VMEM((4, TILE + 2, 3, POINTS), jnp.bfloat16),
            pltpu.VMEM((4, TILE + 2, FEATURES, POINTS), jnp.float32),
            columns, columns,
            pltpu.VMEM((4, TILE + 2, RANK, RANK), jnp.bfloat16),
            pltpu.VMEM((2, TILE, POINTS, RANK), jnp.bfloat16),
            pltpu.VMEM((mine, SLOTS, POINTS, POINTS), jnp.bfloat16),
            pltpu.VMEM((POINTS, POINTS), jnp.bfloat16),
            pltpu.VMEM((POINTS, POINTS), jnp.bfloat16),
            pltpu.VMEM((mine, POINTS, FEATURES), jnp.float32),
            tall, tall, square, square,
            pltpu.VMEM((PANEL, mine, RANK), jnp.float32),
            pltpu.VMEM((mine, 8, RANK), jnp.float32),
            pltpu.VMEM((mine, RANK, POINTS), jnp.bfloat16),
            pltpu.VMEM((mine, SLOTS, RANK, RANK), jnp.float32),
            dma((4,)), dma, dma((2,)), dma((2,)), dma((8,)), dma((8,)), dma((8,)), dma((8,)),
            dma((8,)), dma((8,)), dma((8,)), dma((8,)), dma((2,)), dma((2,)), dma, dma,
        ],
        compiler_params=pltpu.CompilerParams(collective_id=0, has_side_effects=True, vmem_limit_bytes=LIMIT),
        name="plate_level",
    )(near_mask, points, sketch)


def solution(mesh):
    plate = math.isqrt(mesh.shape["box"])

    def step(points, sketch, near_mask):
        return body(plate, points, sketch, near_mask)

    return jax.shard_map(
        step,
        mesh=mesh,
        in_specs=(P("box", None, None), P("box", "col", None), P("box", None)),
        out_specs=(P("box", "col", None), P("box", None, "col", None)),
        check_vma=False,
    )
```

```python
import functools
import math

import jax
import jax.numpy as jnp
from jax import lax
from jax.experimental import pallas as pl
from jax.experimental.pallas import tpu as pltpu
from jax.sharding import PartitionSpec as P

MESH = pl.DeviceIdType.MESH
HIGHEST = lax.Precision.HIGHEST
TILE = 4
POINTS = 512
RANK = 128
FEATURES = 8
SCALE = math.sqrt(8192.0)
SLOTS = 9
LIMIT = 63 << 20
PANEL = 16
NT = (((1,), (1,)), ((), ()))
TN = (((0,), (0,)), ((), ()))
DIRECTIONS = [(dy, dx) for dy in (-1, 0, 1) for dx in (-1, 0, 1) if (dy, dx) != (0, 0)]


def place(step, side, low, high):
    if step == -1:
        return low
    if step == 1:
        return high
    return slice(1, side + 1)


class Halo:
    def __init__(self, plate):
        self.plate = plate
        box, self.col = lax.axis_index("box"), lax.axis_index("col")
        self.row = box // plate * 2 + self.col
        self.column = box % plate
        self.partner = (box, 1 - self.col)

    def device(self, dy, dx):
        high = self.plate * 2
        row = (self.row + dy + high) % high
        column = (self.column + dx + self.plate) % self.plate
        return (row // 2 * self.plate + column, row % 2)

    def barrier(self):
        sem = pltpu.get_barrier_semaphore()
        for dy, dx in DIRECTIONS:
            pl.semaphore_signal(sem, inc=1, device_id=self.device(dy, dx), device_id_type=MESH)
        pl.semaphore_wait(sem, len(DIRECTIONS))

    def copies(self, own, at, ext, send, recv):
        made = []
        for n, (dy, dx) in enumerate(DIRECTIONS):
            rows = (slice(at, at + 2), at, at + 1)
            columns = (slice(at, at + TILE), at, at + TILE - 1)
            made.append(
                pltpu.make_async_remote_copy(
                    src_ref=own.at[rows[0 if dy == 0 else (3 + dy) // 2], columns[0 if dx == 0 else (3 + dx) // 2]],
                    dst_ref=ext.at[place(dy, 2, 3, 0), place(dx, TILE, TILE + 1, 0)],
                    send_sem=send.at[n],
                    recv_sem=recv.at[n],
                    device_id=self.device(dy, dx),
                    device_id_type=MESH,
                )
            )
        return made


def await_row(halo, near_core, ext, send, recv):
    side = halo.col if near_core else 1 - halo.col
    for n, columns in enumerate((TILE + 1, slice(1, TILE + 1), 0)):
        landed = ext.at[3 * (1 - side), columns]
        pltpu.make_async_remote_copy(
            src_ref=landed,
            dst_ref=landed,
            send_sem=send.at[5 * side + n],
            recv_sem=recv.at[5 * side + n],
            device_id=halo.partner,
            device_id_type=MESH,
        ).wait_recv()


def parts(value, count):
    made = []
    for _ in range(count):
        made.append(value.astype(jnp.bfloat16))
        value = value - made[-1].astype(jnp.float32)
    return made


def features(points):
    wide = points.astype(jnp.float32)
    u, v = (wide[0:1] - 0.5) * SCALE, (wide[1:2] - 0.5) * SCALE
    h = (wide[2:3] - 0.5) * (0.25 * SCALE)
    at = lax.broadcasted_iota(jnp.int32, (FEATURES, POINTS), 0)
    rest = jnp.where(at == 2, h, u * u + v * v + h * h)
    return jnp.where(at == 0, u, jnp.where(at == 1, v, rest))


def eliminate(a_ref, p_ref, panel_ref):
    boxes, rank = a_ref.shape[0], a_ref.shape[1]
    lane = lax.broadcasted_iota(jnp.int32, (boxes, rank), 1)
    row_id = lax.broadcasted_iota(jnp.int32, (rank, rank), 0)
    col_id = lax.broadcasted_iota(jnp.int32, (rank, rank), 1)

    def panel(n, carry):
        first = pl.multiple_of(n * PANEL, PANEL)
        for b in range(boxes):
            panel_ref[:, b, :] = a_ref[b, pl.ds(first, PANEL), :]
        rows = [panel_ref[i] for i in range(PANEL)]
        for k in range(0, PANEL, 2):
            here, there = lane == first + k, lane == first + k + 1
            both = here | there
            index = jnp.full((boxes, rank), first + k, jnp.int32)
            upper, lower = rows[k], rows[k + 1]
            p = jnp.take_along_axis(upper, index, axis=1)
            q = jnp.take_along_axis(lower, index, axis=1)
            s = jnp.take_along_axis(lower, index + 1, axis=1)
            det = p * s - q * q
            ratio = 1.0 / p
            last = (1.0 / det) * p
            share = q * ratio
            upper = jnp.where(both, jnp.where(here, 1.0, 0.0), upper)
            lower = jnp.where(both, jnp.where(there, 1.0, 0.0), lower) - share * upper
            x, y = upper * ratio, lower * last
            for i in range(k + 2, PANEL):
                f = jnp.take_along_axis(rows[i], index, axis=1)
                g = jnp.take_along_axis(rows[i], index + 1, axis=1) - f * share
                rows[i] = (jnp.where(both, 0.0, rows[i]) - f * x) - g * y
            outside = (lane < first) | (lane >= first + PANEL)
            rows[k] = jnp.where(outside | (lane <= first + k), upper, 0.0) * lax.rsqrt(p)
            rows[k + 1] = jnp.where(outside | (lane <= first + k + 1), lower, 0.0) * lax.sqrt(last)
        for i in range(PANEL):
            panel_ref[i] = rows[i]
        below = row_id >= first + PANEL
        inside = (col_id >= first) & (col_id < first + PANEL)
        for b in range(boxes):
            own = panel_ref[:, b, :]
            p_ref[b, pl.ds(first, PANEL), :] = jnp.where(col_id[:PANEL] <= row_id[:PANEL] + first, own, 0.0)
            w1, w2, w3 = parts(own, 3)
            left = jnp.concatenate([w1, w1, w2, w1, w2, w3], 0)
            right = jnp.concatenate([w1, w2, w1, w3, w2, w1], 0)
            update = lax.dot_general(left, right, TN, preferred_element_type=jnp.float32)
            old = a_ref[b]
            a_ref[b] = jnp.where(below, jnp.where(inside, 0.0, old) - update, old)
        return carry

    lax.fori_loop(0, rank // PANEL, panel, 0)


def block_of(t, own):
    marks = [t // 40, (t + 22) // 72, (t + 20) // 72, (t + 12) // 72]
    p = t % 10
    some, last = (p + 6) // 10, (p + 3) // 10
    c, x = p - 4 * some - 2 * last, some - 2 * last
    r = t // 20
    steps = [(r, c, t % 20 // 10 * (1 - 2 * r), x), (1 - own, c, 1 - 2 * own, x)]
    n = t - 50
    steps.append((1 - own, 3 * n, 1 - 2 * own, 2 * n - 1))
    n = t - 52
    r, right = n // 4, n // 2 % 2
    steps.append((r, 3 * right, n % 2 * (1 - 2 * r), 2 * right - 1))
    n = t - 60
    steps.append((own, n // 3, 2 * own - 1, n % 3 - 1))
    r, c, y, x = steps[0]
    for mark, before, after in zip(marks, steps, steps[1:]):
        r, c, y, x = [now + mark * (b - a) for now, a, b in zip((r, c, y, x), before, after)]
    return r * TILE + c, 3 * (y + 1) + x + 1


def pair_of(u):
    below, down, back = (u + 10) // 16, (u + 6) // 16, (u + 3) // 16
    r = u // 3 * (1 - below)
    c = u % 3 * (1 - below) + (u - 6) * (below - down) + (u - 10) * (down - back) + (u - 12) * back
    x = 1 - below + down - 2 * back
    return r * TILE + c, 3 * (below + 1) + x + 1


def kernel(
    plate, mask_ref, points_ref, sketch_ref, basis_ref, coupling_ref,
    ext_p, ext_e, ext_o, ext_b, ext_d, rough, kbuf, even, odd, turned, y_ref, work, a_ref, p_ref, panel_ref, scale_ref, basis_t, stage,
    local_sem, out_sem, swap_send, swap_recv, p_send, p_recv, o_send, o_recv,
    b_send, b_recv, d_send, d_recv, half_send, half_recv, c_send, c_recv,
):
    halo = Halo(plate)
    own, other = halo.col, 1 - halo.col
    half = sketch_ref.shape[1]
    rank_half = coupling_ref.shape[2]
    inner = slice(1, TILE + 1)
    mine = pl.ds(pl.multiple_of(own * half, half), half)
    theirs = pl.ds(pl.multiple_of(other * half, half), half)
    locals_p, locals_o, swaps = [], [], []
    for r in range(2):
        boxes = pl.ds(own * 8 + r * TILE, TILE)
        away = pl.ds(other * 8 + r * TILE, TILE)
        locals_p.append(pltpu.make_async_copy(points_ref.at[boxes], ext_p.at[1 + r, inner], local_sem.at[r]))
        locals_o.append(
            pltpu.make_async_copy(sketch_ref.at[boxes], ext_o.at[1 + r, inner, mine], local_sem.at[2 + r])
        )
        swaps.append(
            pltpu.make_async_remote_copy(
                src_ref=sketch_ref.at[away],
                dst_ref=ext_o.at[1 + r, inner, mine],
                send_sem=swap_send.at[r],
                recv_sem=swap_recv.at[r],
                device_id=halo.partner,
                device_id_type=MESH,
            )
        )
    for copy in locals_p + locals_o:
        copy.start()
    halo.barrier()
    for copy in swaps:
        copy.start()
    for copy in locals_p:
        copy.wait()
    p_copies = halo.copies(ext_p, 1, ext_p, p_send, p_recv)
    for copy in p_copies:
        copy.start()

    def own_features(b, carry):
        r, c = 1 + b // TILE, 1 + b % TILE
        value = features(ext_p[r, c])
        ext_e[r, c] = value
        turned[b] = jnp.transpose(value)
        return carry

    lax.fori_loop(0, 8, own_features, 0)
    for copy in locals_o:
        copy.wait()
    for copy in swaps:
        copy.wait_recv()
    o_copies = halo.copies(ext_o, 1, ext_o, o_send, o_recv)
    for copy in o_copies:
        copy.start()

    def weight_of(b, slot):
        return mask_ref[own * 8 + b, slot].astype(jnp.float32)

    def first_term(b, carry):
        y_ref[b] = ext_o[1 + b // TILE, 1 + b % TILE].astype(jnp.float32) * weight_of(b, 4)
        return carry

    lax.fori_loop(0, 8, first_term, 0)

    def fill_block(t, copy_ref):
        b, slot = block_of(t, own)
        near = ext_e[b // TILE + slot // 3, b % TILE + slot % 3]
        u = near[0:1] + (slot % 3 - 1) * SCALE
        v = near[1:2] + (slot // 3 - 1) * SCALE
        h = near[2:3]
        norm = u * u + v * v + h * h + 4.0
        u, v, h = -2.0 * u, -2.0 * v, -2.0 * h
        step = 64
        for first in range(0, POINTS, step):
            rows = slice(first, first + step)
            own_rows = turned[b, rows, :]
            square = (own_rows[:, 3:4] + norm) + own_rows[:, 0:1] * u
            square = square + (own_rows[:, 1:2] * v + own_rows[:, 2:3] * h)
            values = lax.rsqrt(square).astype(jnp.bfloat16)
            kbuf[b, slot, rows, :] = values
            copy_ref[rows, :] = values

    def add_block(t, copy_ref):
        b, slot = block_of(t, own)
        near = ext_o[b // TILE + slot // 3, b % TILE + slot % 3]
        y_ref[b] += jnp.dot(copy_ref[...], near, preferred_element_type=jnp.float32) * weight_of(b, slot)

    def sketch_pair(i, carry):
        t = 2 * i
        add_block(t, even)
        fill_block(t + 1, odd)
        add_block(t + 1, odd)
        fill_block(jnp.minimum(t + 2, 71), even)
        return carry

    def couple_blocks(blocks, mirrored):
        moved = []
        for b, slot in blocks:
            value = jnp.dot(basis_t[b], kbuf[b, slot], preferred_element_type=jnp.float32)
            moved.append(value.astype(jnp.bfloat16))
        for (b, slot), value in zip(blocks, moved):
            y, x = slot // 3 - 1, slot % 3 - 1
            near = ext_b[b // TILE + 1 + y, b % TILE + 1 + x]
            value = jnp.dot(value, near, preferred_element_type=jnp.float32) * (1.0 / POINTS)
            stage[b, slot] = value * weight_of(b, slot)
            start_out(b, slot)
            if mirrored:
                other_b = b + TILE * y + x
                stage[other_b, 8 - slot] = value.T * weight_of(other_b, 8 - slot)
                start_out(other_b, 8 - slot)

    def start_out(b, slot):
        keep, give = out_copies(pl.ds(b, 1), pl.ds(slot, 1), own * 8 + b, 1)
        keep.start()
        give.start()

    def out_copies(b, slot, first, count):
        kept = pl.ds(pl.multiple_of(own * rank_half, rank_half), rank_half)
        given = pl.ds(pl.multiple_of(other * rank_half, rank_half), rank_half)
        target = coupling_ref.at[pl.ds(first, count), slot]
        keep = pltpu.make_async_copy(stage.at[b, slot, kept], target, out_sem)
        give = pltpu.make_async_remote_copy(
            src_ref=stage.at[b, slot, given],
            dst_ref=target,
            send_sem=c_send,
            recv_sem=c_recv,
            device_id=halo.partner,
            device_id_type=MESH,
        )
        return keep, give

    fill_block(0, even)
    lax.fori_loop(0, 19, sketch_pair, 0)
    for copy in p_copies:
        copy.wait_recv()

    def halo_features(t, carry):
        r, c = t // 6, t % 6
        ext_e[3 * r, c] = features(ext_p[3 * r, c])
        return carry

    lax.fori_loop(0, 12, halo_features, 0)

    def side_features(t, carry):
        r, c = 1 + t // 2, t % 2 * (TILE + 1)
        ext_e[r, c] = features(ext_p[r, c])
        return carry

    lax.fori_loop(0, 4, side_features, 0)
    await_row(halo, True, ext_o, o_send, o_recv)
    lax.fori_loop(19, 25, sketch_pair, 0)
    for copy in o_copies[3:5]:
        copy.wait_recv()
    lax.fori_loop(25, 30, sketch_pair, 0)
    await_row(halo, False, ext_o, o_send, o_recv)
    lax.fori_loop(30, 36, sketch_pair, 0)

    def add_units(b, carry):
        same = lax.broadcasted_iota(jnp.int32, (128, 128), 0) == lax.broadcasted_iota(jnp.int32, (128, 128), 1)
        unit = jnp.where(same, 1.0, 0.0)
        for first in range(0, POINTS, 128):
            part = slice(first, first + 128)
            kbuf[b, 4, part, part] = (kbuf[b, 4, part, part].astype(jnp.float32) + unit).astype(jnp.bfloat16)
        return carry

    lax.fori_loop(0, 8, add_units, 0)

    def first_gram(b, carry):
        value = y_ref[b]
        gram = lax.dot_general(value, value, TN, precision=HIGHEST, preferred_element_type=jnp.float32)
        at = [lax.broadcasted_iota(jnp.int32, (RANK, RANK), axis) for axis in (0, 1)]
        diagonal = jnp.where(at[0] == at[1], gram, 0.0)
        along, across = [lax.rsqrt(jnp.sum(diagonal, axis=axis, keepdims=True)) for axis in (0, 1)]
        a_ref[b] = gram * along * across
        scale_ref[b] = jnp.broadcast_to(along * math.sqrt(POINTS), (8, RANK))
        return carry

    def first_apply(b, carry):
        value = lax.dot_general(
            y_ref[b], p_ref[b] * scale_ref[b, 0:1], NT, precision=HIGHEST, preferred_element_type=jnp.float32
        )
        work[b] = value
        rough[b // TILE, b % TILE] = value.astype(jnp.bfloat16)
        return carry

    def second_gram(b, carry):
        high, low = parts(work[b], 2)
        cross = lax.dot_general(high, low, TN, preferred_element_type=jnp.float32)
        gram = lax.dot_general(high, high, TN, preferred_element_type=jnp.float32) + (cross + cross.T)
        a_ref[b] = gram * (1.0 / POINTS)
        return carry

    def second_apply(b, carry):
        high, low = parts(work[b], 2)
        p_high, p_low = parts(p_ref[b], 2)
        value = lax.dot_general(high, p_high, NT, preferred_element_type=jnp.float32)
        value += lax.dot_general(high, p_low, NT, preferred_element_type=jnp.float32)
        value += lax.dot_general(low, p_high, NT, preferred_element_type=jnp.float32)
        ext_b[1 + b // TILE, 1 + b % TILE] = value.astype(jnp.bfloat16)
        return carry

    lax.fori_loop(0, 8, first_gram, 0)
    eliminate(a_ref, p_ref, panel_ref)
    lax.fori_loop(0, 8, first_apply, 0)
    lax.fori_loop(0, 8, second_gram, 0)
    b_copies = halo.copies(rough, 0, ext_b, b_send, b_recv)
    for copy in b_copies:
        copy.start()
    eliminate(a_ref, p_ref, panel_ref)

    def step_of(b, carry):
        at = [lax.broadcasted_iota(jnp.int32, (RANK, RANK), axis) for axis in (0, 1)]
        step = p_ref[b] - jnp.where(at[0] == at[1], 1.0, 0.0)
        ext_d[1 + b // TILE, 1 + b % TILE] = step.astype(jnp.bfloat16)
        return carry

    lax.fori_loop(0, 8, step_of, 0)
    lax.fori_loop(0, 8, second_apply, 0)
    d_copies = halo.copies(ext_d, 1, ext_d, d_send, d_recv)
    for copy in d_copies:
        copy.start()

    def turn_basis(b, carry):
        value = ext_b[1 + b // TILE, 1 + b % TILE].astype(jnp.float32)
        basis_t[b] = jnp.transpose(value).astype(jnp.bfloat16)
        return carry

    lax.fori_loop(0, 8, turn_basis, 0)
    keeps, gives = [], []
    for r in range(2):
        boxes = pl.ds(own * 8 + r * TILE, TILE)
        keeps.append(
            pltpu.make_async_copy(ext_b.at[1 + r, inner, mine], basis_ref.at[boxes], local_sem.at[r])
        )
        gives.append(
            pltpu.make_async_remote_copy(
                src_ref=ext_b.at[1 + r, inner, theirs],
                dst_ref=basis_ref.at[boxes],
                send_sem=half_send.at[r],
                recv_sem=half_recv.at[r],
                device_id=halo.partner,
                device_id_type=MESH,
            )
        )
    for copy in keeps + gives:
        copy.start()

    def couple_centres(i, carry):
        couple_blocks([(2 * i, 4), (2 * i + 1, 4)], False)
        return carry

    def couple_pairs(i, carry):
        couple_blocks([pair_of(2 * i), pair_of(2 * i + 1)], True)
        return carry

    def couple_rest(i, carry):
        couple_blocks([block_of(2 * i, own), block_of(2 * i + 1, own)], False)
        return carry

    lax.fori_loop(0, 4, couple_centres, 0)
    lax.fori_loop(0, 8, couple_pairs, 0)

    def finish_near(r, c):
        near = ext_b[r, c]
        change = lax.dot_general(near, ext_d[r, c], NT, preferred_element_type=jnp.float32)
        ext_b[r, c] = (near.astype(jnp.float32) + change).astype(jnp.bfloat16)

    def finish_row(row):
        def finish(c, carry):
            finish_near(row, c)
            return carry

        lax.fori_loop(0, TILE + 2, finish, 0)

    def finish_side(t, carry):
        finish_near(1 + t // 2, t % 2 * (TILE + 1))
        return carry

    await_row(halo, True, ext_b, b_send, b_recv)
    await_row(halo, True, ext_d, d_send, d_recv)
    for copy in b_copies[3:5] + d_copies[3:5]:
        copy.wait_recv()
    finish_row(3 * (1 - own))
    lax.fori_loop(0, 4, finish_side, 0)
    lax.fori_loop(20, 30, couple_rest, 0)
    await_row(halo, False, ext_b, b_send, b_recv)
    await_row(halo, False, ext_d, d_send, d_recv)
    finish_row(3 * own)
    lax.fori_loop(30, 36, couple_rest, 0)
    keep, give = out_copies(slice(None), slice(None), own * 8, 8)
    keep.wait()
    give.wait()
    for copy in keeps + gives:
        copy.wait()
    for copy in swaps + p_copies + o_copies + b_copies + d_copies:
        copy.wait_send()


def body(plate, points, sketch, near_mask):
    boxes = points.shape[0]
    mine = boxes // 2
    hbm, smem = (pl.BlockSpec(memory_space=space) for space in (pl.ANY, pltpu.SMEM))
    dma = pltpu.SemaphoreType.DMA
    columns = pltpu.VMEM((4, TILE + 2, POINTS, RANK), jnp.bfloat16)
    tall = pltpu.VMEM((mine, POINTS, RANK), jnp.float32)
    square = pltpu.VMEM((mine, RANK, RANK), jnp.float32)
    return pl.pallas_call(
        functools.partial(kernel, plate),
        out_shape=(
            jax.ShapeDtypeStruct((boxes, POINTS // 2, RANK), jnp.bfloat16),
            jax.ShapeDtypeStruct((boxes, SLOTS, RANK // 2, RANK), jnp.float32),
        ),
        in_specs=[smem, hbm, hbm],
        out_specs=(hbm, hbm),
        scratch_shapes=[
            pltpu.VMEM((4, TILE + 2, 3, POINTS), jnp.bfloat16),
            pltpu.VMEM((4, TILE + 2, FEATURES, POINTS), jnp.float32),
            columns, columns,
            pltpu.VMEM((4, TILE + 2, RANK, RANK), jnp.bfloat16),
            pltpu.VMEM((2, TILE, POINTS, RANK), jnp.bfloat16),
            pltpu.VMEM((mine, SLOTS, POINTS, POINTS), jnp.bfloat16),
            pltpu.VMEM((POINTS, POINTS), jnp.bfloat16),
            pltpu.VMEM((POINTS, POINTS), jnp.bfloat16),
            pltpu.VMEM((mine, POINTS, FEATURES), jnp.float32),
            tall, tall, square, square,
            pltpu.VMEM((PANEL, mine, RANK), jnp.float32),
            pltpu.VMEM((mine, 8, RANK), jnp.float32),
            pltpu.VMEM((mine, RANK, POINTS), jnp.bfloat16),
            pltpu.VMEM((mine, SLOTS, RANK, RANK), jnp.float32),
            dma((4,)), dma, dma((2,)), dma((2,)), dma((8,)), dma((8,)), dma((8,)), dma((8,)),
            dma((8,)), dma((8,)), dma((8,)), dma((8,)), dma((2,)), dma((2,)), dma, dma,
        ],
        compiler_params=pltpu.CompilerParams(collective_id=0, has_side_effects=True, vmem_limit_bytes=LIMIT),
        name="plate_level",
    )(near_mask, points, sketch)


def solution(mesh):
    plate = math.isqrt(mesh.shape["box"])

    def step(points, sketch, near_mask):
        return body(plate, points, sketch, near_mask)

    return jax.shard_map(
        step,
        mesh=mesh,
        in_specs=(P("box", None, None), P("box", "col", None), P("box", None)),
        out_specs=(P("box", "col", None), P("box", None, "col", None)),
        check_vma=False,
    )
```

```python
import functools
import math

import jax
import jax.numpy as jnp
from jax import lax
from jax.experimental import pallas as pl
from jax.experimental.pallas import tpu as pltpu
from jax.sharding import PartitionSpec as P

MESH = pl.DeviceIdType.MESH
TILE = 4
POINTS = 512
RANK = 128
FEATURES = 8
SCALE = math.sqrt(8192.0)
SLOTS = 9
LIMIT = 63 << 20
PANEL = 16
NT = (((1,), (1,)), ((), ()))
TN = (((0,), (0,)), ((), ()))
PAIRS = (
    [[(c, 7) for c in range(4)]]
    + [[(c, 5), (4 + c, 5), (c, 8), (c + 1, 6)] for c in range(3)]
)
DIRECTIONS = [(dy, dx) for dy in (-1, 0, 1) for dx in (-1, 0, 1) if (dy, dx) != (0, 0)]


def place(step, side, low, high):
    if step == -1:
        return low
    if step == 1:
        return high
    return slice(1, side + 1)


class Halo:
    def __init__(self, plate):
        self.plate = plate
        box, self.col = lax.axis_index("box"), lax.axis_index("col")
        self.row = box // plate * 2 + self.col
        self.column = box % plate
        self.partner = (box, 1 - self.col)

    def device(self, dy, dx):
        high = self.plate * 2
        row = (self.row + dy + high) % high
        column = (self.column + dx + self.plate) % self.plate
        return (row // 2 * self.plate + column, row % 2)

    def barrier(self):
        sem = pltpu.get_barrier_semaphore()
        for dy, dx in DIRECTIONS:
            pl.semaphore_signal(sem, inc=1, device_id=self.device(dy, dx), device_id_type=MESH)
        pl.semaphore_wait(sem, len(DIRECTIONS))

    def copies(self, own, at, ext, send, recv):
        made = []
        for n, (dy, dx) in enumerate(DIRECTIONS):
            rows = (slice(at, at + 2), at, at + 1)
            columns = (slice(at, at + TILE), at, at + TILE - 1)
            made.append(
                pltpu.make_async_remote_copy(
                    src_ref=own.at[rows[0 if dy == 0 else (3 + dy) // 2], columns[0 if dx == 0 else (3 + dx) // 2]],
                    dst_ref=ext.at[place(dy, 2, 3, 0), place(dx, TILE, TILE + 1, 0)],
                    send_sem=send.at[n],
                    recv_sem=recv.at[n],
                    device_id=self.device(dy, dx),
                    device_id_type=MESH,
                )
            )
        return made


def await_row(halo, near_core, ext, send, recv):
    side = halo.col if near_core else 1 - halo.col
    for n, columns in enumerate((TILE + 1, slice(1, TILE + 1), 0)):
        landed = ext.at[3 * (1 - side), columns]
        pltpu.make_async_remote_copy(
            src_ref=landed,
            dst_ref=landed,
            send_sem=send.at[5 * side + n],
            recv_sem=recv.at[5 * side + n],
            device_id=halo.partner,
            device_id_type=MESH,
        ).wait_recv()


def parts(value, count):
    made = []
    for _ in range(count):
        made.append(value.astype(jnp.bfloat16))
        value = value - made[-1].astype(jnp.float32)
    return made


def features(points):
    wide = points.astype(jnp.float32)
    u, v = (wide[0:1] - 0.5) * SCALE, (wide[1:2] - 0.5) * SCALE
    h = (wide[2:3] - 0.5) * (0.25 * SCALE)
    at = lax.broadcasted_iota(jnp.int32, (FEATURES, POINTS), 0)
    rest = jnp.where(at == 2, h, u * u + v * v + h * h)
    return jnp.where(at == 0, u, jnp.where(at == 1, v, rest))


def eliminate(a_ref, p_ref, panel_ref):
    boxes, rank = a_ref.shape[0], a_ref.shape[1]
    lane = lax.broadcasted_iota(jnp.int32, (boxes, rank), 1)
    row_id = lax.broadcasted_iota(jnp.int32, (rank, rank), 0)
    col_id = lax.broadcasted_iota(jnp.int32, (rank, rank), 1)

    def panel(n, carry):
        first = pl.multiple_of(n * PANEL, PANEL)
        for b in range(boxes):
            panel_ref[:, b, :] = a_ref[b, pl.ds(first, PANEL), :]
        rows = [panel_ref[i] for i in range(PANEL)]
        for k in range(0, PANEL, 2):
            here, there = lane == first + k, lane == first + k + 1
            both = here | there
            index = jnp.full((boxes, rank), first + k, jnp.int32)
            upper, lower = rows[k], rows[k + 1]
            p = jnp.take_along_axis(upper, index, axis=1)
            q = jnp.take_along_axis(lower, index, axis=1)
            s = jnp.take_along_axis(lower, index + 1, axis=1)
            det = p * s - q * q
            ratio = 1.0 / p
            last = (1.0 / det) * p
            share = q * ratio
            upper = jnp.where(both, jnp.where(here, 1.0, 0.0), upper)
            lower = jnp.where(both, jnp.where(there, 1.0, 0.0), lower) - share * upper
            x, y = upper * ratio, lower * last
            for i in range(k + 2, PANEL):
                f = jnp.take_along_axis(rows[i], index, axis=1)
                g = jnp.take_along_axis(rows[i], index + 1, axis=1) - f * share
                rows[i] = (jnp.where(both, 0.0, rows[i]) - f * x) - g * y
            outside = (lane < first) | (lane >= first + PANEL)
            rows[k] = jnp.where(outside | (lane <= first + k), upper, 0.0) * lax.rsqrt(p)
            rows[k + 1] = jnp.where(outside | (lane <= first + k + 1), lower, 0.0) * lax.sqrt(last)
        for i in range(PANEL):
            panel_ref[i] = rows[i]
        below = row_id >= first + PANEL
        inside = (col_id >= first) & (col_id < first + PANEL)
        for b in range(boxes):
            own = panel_ref[:, b, :]
            p_ref[b, pl.ds(first, PANEL), :] = jnp.where(col_id[:PANEL] <= row_id[:PANEL] + first, own, 0.0)
            w1, w2, w3 = parts(own, 3)
            left = jnp.concatenate([w1, w1, w2, w1, w2, w3], 0)
            right = jnp.concatenate([w1, w2, w1, w3, w2, w1], 0)
            update = lax.dot_general(left, right, TN, preferred_element_type=jnp.float32)
            old = a_ref[b]
            a_ref[b] = jnp.where(below, jnp.where(inside, 0.0, old) - update, old)
        return carry

    lax.fori_loop(0, rank // PANEL, panel, 0)


def block_of(t, own):
    marks = [t // 40, (t + 22) // 72, (t + 20) // 72, (t + 12) // 72]
    p = t % 10
    some, last = (p + 6) // 10, (p + 3) // 10
    c, x = p - 4 * some - 2 * last, some - 2 * last
    r = t // 20
    steps = [(r, c, t % 20 // 10 * (1 - 2 * r), x), (1 - own, c, 1 - 2 * own, x)]
    n = t - 50
    steps.append((1 - own, 3 * n, 1 - 2 * own, 2 * n - 1))
    n = t - 52
    r, right = n // 4, n // 2 % 2
    steps.append((r, 3 * right, n % 2 * (1 - 2 * r), 2 * right - 1))
    n = t - 60
    steps.append((own, n // 3, 2 * own - 1, n % 3 - 1))
    r, c, y, x = steps[0]
    for mark, before, after in zip(marks, steps, steps[1:]):
        r, c, y, x = [now + mark * (b - a) for now, a, b in zip((r, c, y, x), before, after)]
    return r * TILE + c, 3 * (y + 1) + x + 1


def full_gram(value):
    a, b, c = parts(value, 3)
    rank = value.shape[1]
    wide = lax.dot_general(a, jnp.concatenate([a, b], 1), TN, preferred_element_type=jnp.float32)
    rest = lax.dot_general(
        jnp.concatenate([a, b], 0), jnp.concatenate([c, b * 0.5], 0), TN, preferred_element_type=jnp.float32
    )
    cross = wide[:, rank:] + rest
    return wide[:, :rank] + (cross + cross.T)


def full_apply(value, factor):
    a, b, c = parts(value, 3)
    p, q, r = parts(factor, 3)
    rank = value.shape[1]
    right = jnp.concatenate([jnp.concatenate([p, p], 1), jnp.concatenate([q, q], 1)], 0)
    wide = lax.dot_general(jnp.concatenate([a, b], 1), right, NT, preferred_element_type=jnp.float32)
    rest = lax.dot_general(
        jnp.concatenate([c, a], 1), jnp.concatenate([p, r], 1), NT, preferred_element_type=jnp.float32
    )
    return wide[:, :rank] + (wide[:, rank:] + rest)


def near_gram(value):
    a, b = parts(value, 2)
    rank = value.shape[1]
    wide = lax.dot_general(a, jnp.concatenate([a, b], 1), TN, preferred_element_type=jnp.float32)
    cross = wide[:, rank:]
    return wide[:, :rank] + (cross + cross.T)


def near_apply(value, factor):
    a, b = parts(value, 2)
    p, q = parts(factor, 2)
    rank = value.shape[1]
    right = jnp.concatenate([jnp.concatenate([p, p], 1), jnp.concatenate([q, jnp.zeros_like(q)], 1)], 0)
    wide = lax.dot_general(jnp.concatenate([a, b], 1), right, NT, preferred_element_type=jnp.float32)
    return wide[:, :rank] + wide[:, rank:]


def kernel(
    plate, mask_ref, points_ref, sketch_ref, basis_ref, coupling_ref,
    ext_p, ext_e, ext_o, ext_b, ext_d, rough, kbuf, even, odd, turned, y_ref, work, a_ref, p_ref, panel_ref, scale_ref, basis_t, stage,
    local_sem, out_sem, swap_send, swap_recv, p_send, p_recv, o_send, o_recv,
    b_send, b_recv, d_send, d_recv, half_send, half_recv, c_send, c_recv,
):
    halo = Halo(plate)
    own, other = halo.col, 1 - halo.col
    half = sketch_ref.shape[1]
    rank_half = coupling_ref.shape[2]
    inner = slice(1, TILE + 1)
    mine = pl.ds(pl.multiple_of(own * half, half), half)
    theirs = pl.ds(pl.multiple_of(other * half, half), half)
    locals_p, locals_o, swaps = [], [], []
    for r in range(2):
        boxes = pl.ds(own * 8 + r * TILE, TILE)
        away = pl.ds(other * 8 + r * TILE, TILE)
        locals_p.append(pltpu.make_async_copy(points_ref.at[boxes], ext_p.at[1 + r, inner], local_sem.at[r]))
        locals_o.append(
            pltpu.make_async_copy(sketch_ref.at[boxes], ext_o.at[1 + r, inner, mine], local_sem.at[2 + r])
        )
        swaps.append(
            pltpu.make_async_remote_copy(
                src_ref=sketch_ref.at[away],
                dst_ref=ext_o.at[1 + r, inner, mine],
                send_sem=swap_send.at[r],
                recv_sem=swap_recv.at[r],
                device_id=halo.partner,
                device_id_type=MESH,
            )
        )
    for copy in locals_p + locals_o:
        copy.start()
    halo.barrier()
    for copy in swaps:
        copy.start()
    for copy in locals_p:
        copy.wait()
    p_copies = halo.copies(ext_p, 1, ext_p, p_send, p_recv)
    for copy in p_copies:
        copy.start()

    def own_features(b, carry):
        r, c = 1 + b // TILE, 1 + b % TILE
        value = features(ext_p[r, c])
        ext_e[r, c] = value
        turned[b] = jnp.transpose(value)
        return carry

    lax.fori_loop(0, 8, own_features, 0)
    for copy in locals_o:
        copy.wait()
    for copy in swaps:
        copy.wait_recv()
    o_copies = halo.copies(ext_o, 1, ext_o, o_send, o_recv)
    for copy in o_copies:
        copy.start()

    def weight_of(b, slot):
        return mask_ref[own * 8 + b, slot].astype(jnp.float32)

    def first_term(b, carry):
        y_ref[b] = ext_o[1 + b // TILE, 1 + b % TILE].astype(jnp.float32) * weight_of(b, 4)
        return carry

    lax.fori_loop(0, 8, first_term, 0)

    def fill_block(t, copy_ref):
        b, slot = block_of(t, own)
        near = ext_e[b // TILE + slot // 3, b % TILE + slot % 3]
        u = near[0:1] + (slot % 3 - 1) * SCALE
        v = near[1:2] + (slot // 3 - 1) * SCALE
        h = near[2:3]
        norm = u * u + v * v + h * h + 4.0
        u, v, h = -2.0 * u, -2.0 * v, -2.0 * h
        step = 64
        for first in range(0, POINTS, step):
            rows = slice(first, first + step)
            own_rows = turned[b, rows, :]
            square = (own_rows[:, 3:4] + norm) + own_rows[:, 0:1] * u
            square = square + (own_rows[:, 1:2] * v + own_rows[:, 2:3] * h)
            values = lax.rsqrt(square).astype(jnp.bfloat16)
            kbuf[b, slot, rows, :] = values
            copy_ref[rows, :] = values

    def add_block(t, copy_ref):
        b, slot = block_of(t, own)
        near = ext_o[b // TILE + slot // 3, b % TILE + slot % 3]
        y_ref[b] += jnp.dot(copy_ref[...], near, preferred_element_type=jnp.float32) * weight_of(b, slot)

    def sketch_pair(i, carry):
        t = 2 * i
        add_block(t, even)
        fill_block(t + 1, odd)
        add_block(t + 1, odd)
        fill_block(jnp.minimum(t + 2, 71), even)
        return carry

    def couple_blocks(blocks, mirrored=False, batched=False):
        moved = []
        for b, slot in blocks:
            value = jnp.dot(basis_t[b], kbuf[b, slot], preferred_element_type=jnp.float32)
            moved.append(value.astype(jnp.bfloat16))
        turned_blocks = []
        for (b, slot), value in zip(blocks, moved):
            y, x = slot // 3 - 1, slot % 3 - 1
            near = ext_b[b // TILE + 1 + y, b % TILE + 1 + x]
            value = jnp.dot(value, near, preferred_element_type=jnp.float32) * (1.0 / POINTS)
            stage[b, slot] = (value * weight_of(b, slot)).astype(stage.dtype)
            if mirrored:
                other_b = b + TILE * y + x
                stage[other_b, 8 - slot] = (value.T * weight_of(other_b, 8 - slot)).astype(stage.dtype)
                turned_blocks.append((other_b, 8 - slot))
        for done in (blocks, turned_blocks):
            if batched and done:
                start_out(done[0][0], done[0][1], len(done))
            for b, slot in [] if batched else done:
                start_out(b, slot, 1)

    def start_out(b, slot, count):
        keep, give = out_copies(pl.ds(b, count), pl.ds(slot, 1), own * 8 + b, count)
        keep.start()
        give.start()

    def out_copies(b, slot, first, count):
        kept = pl.ds(pl.multiple_of(own * rank_half, rank_half), rank_half)
        given = pl.ds(pl.multiple_of(other * rank_half, rank_half), rank_half)
        target = coupling_ref.at[pl.ds(first, count), slot]
        keep = pltpu.make_async_copy(stage.at[b, slot, kept], target, out_sem)
        give = pltpu.make_async_remote_copy(
            src_ref=stage.at[b, slot, given],
            dst_ref=target,
            send_sem=c_send,
            recv_sem=c_recv,
            device_id=halo.partner,
            device_id_type=MESH,
        )
        return keep, give

    fill_block(0, even)
    lax.fori_loop(0, 19, sketch_pair, 0)
    for copy in p_copies:
        copy.wait_recv()

    def halo_features(t, carry):
        r, c = t // 6, t % 6
        ext_e[3 * r, c] = features(ext_p[3 * r, c])
        return carry

    lax.fori_loop(0, 12, halo_features, 0)

    def side_features(t, carry):
        r, c = 1 + t // 2, t % 2 * (TILE + 1)
        ext_e[r, c] = features(ext_p[r, c])
        return carry

    lax.fori_loop(0, 4, side_features, 0)
    await_row(halo, True, ext_o, o_send, o_recv)
    lax.fori_loop(19, 25, sketch_pair, 0)
    for copy in o_copies[3:5]:
        copy.wait_recv()
    lax.fori_loop(25, 30, sketch_pair, 0)
    await_row(halo, False, ext_o, o_send, o_recv)
    lax.fori_loop(30, 36, sketch_pair, 0)

    def add_units(b, carry):
        same = lax.broadcasted_iota(jnp.int32, (128, 128), 0) == lax.broadcasted_iota(jnp.int32, (128, 128), 1)
        unit = jnp.where(same, 1.0, 0.0)
        for first in range(0, POINTS, 128):
            part = slice(first, first + 128)
            kbuf[b, 4, part, part] = (kbuf[b, 4, part, part].astype(jnp.float32) + unit).astype(jnp.bfloat16)
        return carry

    lax.fori_loop(0, 8, add_units, 0)

    def by_fours(step):
        def four(i, carry):
            for n in range(4):
                step(4 * i + n, carry)
            return carry

        lax.fori_loop(0, 2, four, 0)

    def first_gram(b, carry):
        value = y_ref[b]
        gram = full_gram(value)
        at = [lax.broadcasted_iota(jnp.int32, (RANK, RANK), axis) for axis in (0, 1)]
        diagonal = jnp.where(at[0] == at[1], gram, 0.0)
        along, across = [lax.rsqrt(jnp.sum(diagonal, axis=axis, keepdims=True)) for axis in (0, 1)]
        a_ref[b] = gram * along * across
        scale_ref[b] = jnp.broadcast_to(along * math.sqrt(POINTS), (8, RANK))
        return carry

    def first_apply(b, carry):
        value = full_apply(y_ref[b], p_ref[b] * scale_ref[b, 0:1])
        work[b] = value
        rough[b // TILE, b % TILE] = value.astype(jnp.bfloat16)
        return carry

    def second_gram(b, carry):
        a_ref[b] = near_gram(work[b]) * (1.0 / POINTS)
        return carry

    def second_apply(b, carry):
        value = near_apply(work[b], p_ref[b])
        ext_b[1 + b // TILE, 1 + b % TILE] = value.astype(jnp.bfloat16)
        return carry

    by_fours(first_gram)
    eliminate(a_ref, p_ref, panel_ref)
    by_fours(first_apply)
    by_fours(second_gram)
    b_copies = halo.copies(rough, 0, ext_b, b_send, b_recv)
    for copy in b_copies:
        copy.start()
    eliminate(a_ref, p_ref, panel_ref)

    def step_of(b, carry):
        at = [lax.broadcasted_iota(jnp.int32, (RANK, RANK), axis) for axis in (0, 1)]
        step = p_ref[b] - jnp.where(at[0] == at[1], 1.0, 0.0)
        ext_d[1 + b // TILE, 1 + b % TILE] = step.astype(jnp.bfloat16)
        return carry

    lax.fori_loop(0, 8, step_of, 0)
    by_fours(second_apply)
    d_copies = halo.copies(ext_d, 1, ext_d, d_send, d_recv)
    for copy in d_copies:
        copy.start()

    def turn_basis(b, carry):
        value = ext_b[1 + b // TILE, 1 + b % TILE].astype(jnp.float32)
        basis_t[b] = jnp.transpose(value).astype(jnp.bfloat16)
        return carry

    lax.fori_loop(0, 8, turn_basis, 0)
    keeps, gives = [], []
    for r in range(2):
        boxes = pl.ds(own * 8 + r * TILE, TILE)
        keeps.append(
            pltpu.make_async_copy(ext_b.at[1 + r, inner, mine], basis_ref.at[boxes], local_sem.at[r])
        )
        gives.append(
            pltpu.make_async_remote_copy(
                src_ref=ext_b.at[1 + r, inner, theirs],
                dst_ref=basis_ref.at[boxes],
                send_sem=half_send.at[r],
                recv_sem=half_recv.at[r],
                device_id=halo.partner,
                device_id_type=MESH,
            )
        )
    for copy in keeps + gives:
        copy.start()

    def couple_centres(i, carry):
        couple_blocks([(4 * i + n, 4) for n in range(4)], batched=True)
        return carry

    lax.fori_loop(0, 2, couple_centres, 0)
    for n, pairs in enumerate(PAIRS):
        couple_blocks(pairs, mirrored=True, batched=n == 0)

    def couple_across(r, y):
        def body(i, carry):
            couple_blocks([(r * TILE + n, 3 * (y + 1) + i) for n in range(4)], batched=True)
            return carry

        lax.fori_loop(0, 3, body, 0)

    def couple_sides(right, carry):
        couple_blocks([(n // 2 * TILE + 3 * right, 3 * (n % 2 * (1 - n // 2 * 2) + 1) + 2 * right) for n in range(4)])
        return carry

    def finish_near(r, c):
        near = ext_b[r, c]
        change = lax.dot_general(near, ext_d[r, c], NT, preferred_element_type=jnp.float32)
        ext_b[r, c] = (near.astype(jnp.float32) + change).astype(jnp.bfloat16)

    def finish_row(row):
        def finish(c, carry):
            finish_near(row, c)
            return carry

        lax.fori_loop(0, TILE + 2, finish, 0)

    def finish_side(t, carry):
        finish_near(1 + t // 2, t % 2 * (TILE + 1))
        return carry

    await_row(halo, True, ext_b, b_send, b_recv)
    await_row(halo, True, ext_d, d_send, d_recv)
    for copy in b_copies[3:5] + d_copies[3:5]:
        copy.wait_recv()
    finish_row(3 * (1 - own))
    lax.fori_loop(0, 4, finish_side, 0)
    couple_across(1 - own, 1 - 2 * own)
    lax.fori_loop(0, 2, couple_sides, 0)
    await_row(halo, False, ext_b, b_send, b_recv)
    await_row(halo, False, ext_d, d_send, d_recv)
    finish_row(3 * own)
    couple_across(own, 2 * own - 1)
    keep, give = out_copies(slice(None), slice(None), own * 8, 8)
    keep.wait()
    give.wait()
    for copy in keeps + gives:
        copy.wait()
    for copy in swaps + p_copies + o_copies + b_copies + d_copies:
        copy.wait_send()


def body(plate, points, sketch, near_mask):
    boxes = points.shape[0]
    mine = boxes // 2
    hbm, smem = (pl.BlockSpec(memory_space=space) for space in (pl.ANY, pltpu.SMEM))
    dma = pltpu.SemaphoreType.DMA
    columns = pltpu.VMEM((4, TILE + 2, POINTS, RANK), jnp.bfloat16)
    tall = pltpu.VMEM((mine, POINTS, RANK), jnp.float32)
    square = pltpu.VMEM((mine, RANK, RANK), jnp.float32)
    basis, coupling = pl.pallas_call(
        functools.partial(kernel, plate),
        out_shape=(
            jax.ShapeDtypeStruct((boxes, POINTS // 2, RANK), jnp.bfloat16),
            jax.ShapeDtypeStruct((boxes, SLOTS, RANK // 2, RANK), jnp.bfloat16),
        ),
        in_specs=[smem, hbm, hbm],
        out_specs=(hbm, hbm),
        scratch_shapes=[
            pltpu.VMEM((4, TILE + 2, 3, POINTS), jnp.bfloat16),
            pltpu.VMEM((4, TILE + 2, FEATURES, POINTS), jnp.float32),
            columns, columns,
            pltpu.VMEM((4, TILE + 2, RANK, RANK), jnp.bfloat16),
            pltpu.VMEM((2, TILE, POINTS, RANK), jnp.bfloat16),
            pltpu.VMEM((mine, SLOTS, POINTS, POINTS), jnp.bfloat16),
            pltpu.VMEM((POINTS, POINTS), jnp.bfloat16),
            pltpu.VMEM((POINTS, POINTS), jnp.bfloat16),
            pltpu.VMEM((mine, POINTS, FEATURES), jnp.float32),
            tall, tall, square, square,
            pltpu.VMEM((PANEL, mine, RANK), jnp.float32),
            pltpu.VMEM((mine, 8, RANK), jnp.float32),
            pltpu.VMEM((mine, RANK, POINTS), jnp.bfloat16),
            pltpu.VMEM((mine, SLOTS, RANK, RANK), jnp.bfloat16),
            dma((4,)), dma, dma((2,)), dma((2,)), dma((8,)), dma((8,)), dma((8,)), dma((8,)),
            dma((8,)), dma((8,)), dma((8,)), dma((8,)), dma((2,)), dma((2,)), dma, dma,
        ],
        compiler_params=pltpu.CompilerParams(collective_id=0, has_side_effects=True, vmem_limit_bytes=LIMIT),
        name="plate_level",
    )(near_mask, points, sketch)
    return basis, coupling.astype(jnp.float32)


def solution(mesh):
    plate = math.isqrt(mesh.shape["box"])

    def step(points, sketch, near_mask):
        return body(plate, points, sketch, near_mask)

    return jax.shard_map(
        step,
        mesh=mesh,
        in_specs=(P("box", None, None), P("box", "col", None), P("box", None)),
        out_specs=(P("box", "col", None), P("box", None, "col", None)),
        check_vma=False,
    )
```

```python
import functools
import math

import jax
import jax.numpy as jnp
from jax import lax
from jax.experimental import pallas as pl
from jax.experimental.pallas import tpu as pltpu
from jax.sharding import PartitionSpec as P

MESH = pl.DeviceIdType.MESH
TILE = 4
POINTS = 512
RANK = 128
FEATURES = 8
SCALE = math.sqrt(8192.0)
SLOTS = 9
LIMIT = 63 << 20
PANEL = 16
NT = (((1,), (1,)), ((), ()))
TN = (((0,), (0,)), ((), ()))
PAIRS = (
    [[(c, 7) for c in range(4)]]
    + [[(c, 5), (4 + c, 5), (c, 8), (c + 1, 6)] for c in range(3)]
)
DIRECTIONS = [(dy, dx) for dy in (-1, 0, 1) for dx in (-1, 0, 1) if (dy, dx) != (0, 0)]


def place(step, side, low, high):
    if step == -1:
        return low
    if step == 1:
        return high
    return slice(1, side + 1)


class Halo:
    def __init__(self, plate):
        self.plate = plate
        box, self.col = lax.axis_index("box"), lax.axis_index("col")
        self.row = box // plate * 2 + self.col
        self.column = box % plate
        self.partner = (box, 1 - self.col)

    def device(self, dy, dx):
        high = self.plate * 2
        row = (self.row + dy + high) % high
        column = (self.column + dx + self.plate) % self.plate
        return (row // 2 * self.plate + column, row % 2)

    def barrier(self):
        sem = pltpu.get_barrier_semaphore()
        for dy, dx in DIRECTIONS:
            pl.semaphore_signal(sem, inc=1, device_id=self.device(dy, dx), device_id_type=MESH)
        pl.semaphore_wait(sem, len(DIRECTIONS))

    def copies(self, own, at, ext, send, recv):
        made = []
        for n, (dy, dx) in enumerate(DIRECTIONS):
            rows = (slice(at, at + 2), at, at + 1)
            columns = (slice(at, at + TILE), at, at + TILE - 1)
            made.append(
                pltpu.make_async_remote_copy(
                    src_ref=own.at[rows[0 if dy == 0 else (3 + dy) // 2], columns[0 if dx == 0 else (3 + dx) // 2]],
                    dst_ref=ext.at[place(dy, 2, 3, 0), place(dx, TILE, TILE + 1, 0)],
                    send_sem=send.at[n],
                    recv_sem=recv.at[n],
                    device_id=self.device(dy, dx),
                    device_id_type=MESH,
                )
            )
        return made


def row_copies(halo, near_core, own, ext, send, recv):
    row = 1 - halo.col if near_core else halo.col
    dy = 2 * row - 1
    made = []
    for dx in (-1, 0, 1):
        n = 5 * row + dx + 1
        made.append(
            pltpu.make_async_remote_copy(
                src_ref=own.at[row, {-1: 0, 0: slice(0, TILE), 1: TILE - 1}[dx]],
                dst_ref=ext.at[3 * (1 - row), place(dx, TILE, TILE + 1, 0)],
                send_sem=send.at[n],
                recv_sem=recv.at[n],
                device_id=halo.device(dy, dx),
                device_id_type=MESH,
            )
        )
    return made


def await_row(halo, near_core, ext, send, recv):
    side = halo.col if near_core else 1 - halo.col
    for n, columns in enumerate((TILE + 1, slice(1, TILE + 1), 0)):
        landed = ext.at[3 * (1 - side), columns]
        pltpu.make_async_remote_copy(
            src_ref=landed,
            dst_ref=landed,
            send_sem=send.at[5 * side + n],
            recv_sem=recv.at[5 * side + n],
            device_id=halo.partner,
            device_id_type=MESH,
        ).wait_recv()


def parts(value, count):
    made = []
    for _ in range(count):
        made.append(value.astype(jnp.bfloat16))
        value = value - made[-1].astype(jnp.float32)
    return made


def features(points):
    wide = points.astype(jnp.float32)
    u, v = (wide[0:1] - 0.5) * SCALE, (wide[1:2] - 0.5) * SCALE
    h = (wide[2:3] - 0.5) * (0.25 * SCALE)
    at = lax.broadcasted_iota(jnp.int32, (FEATURES, POINTS), 0)
    rest = jnp.where(at == 2, h, u * u + v * v + h * h)
    return jnp.where(at == 0, u, jnp.where(at == 1, v, rest))


def eliminate(a_ref, p_ref, panel_ref):
    boxes, rank = a_ref.shape[0], a_ref.shape[1]
    lane = lax.broadcasted_iota(jnp.int32, (boxes, rank), 1)
    row_id = lax.broadcasted_iota(jnp.int32, (rank, rank), 0)
    col_id = lax.broadcasted_iota(jnp.int32, (rank, rank), 1)

    def panel(n, carry):
        first = pl.multiple_of(n * PANEL, PANEL)
        for b in range(boxes):
            panel_ref[:, b, :] = a_ref[b, pl.ds(first, PANEL), :]
        rows = [panel_ref[i] for i in range(PANEL)]
        for k in range(0, PANEL, 2):
            here, there = lane == first + k, lane == first + k + 1
            both = here | there
            index = jnp.full((boxes, rank), first + k, jnp.int32)
            upper, lower = rows[k], rows[k + 1]
            p = jnp.take_along_axis(upper, index, axis=1)
            q = jnp.take_along_axis(lower, index, axis=1)
            s = jnp.take_along_axis(lower, index + 1, axis=1)
            det = p * s - q * q
            ratio = 1.0 / p
            last = (1.0 / det) * p
            share = q * ratio
            upper = jnp.where(both, jnp.where(here, 1.0, 0.0), upper)
            lower = jnp.where(both, jnp.where(there, 1.0, 0.0), lower) - share * upper
            x, y = upper * ratio, lower * last
            for i in range(k + 2, PANEL):
                f = jnp.take_along_axis(rows[i], index, axis=1)
                g = jnp.take_along_axis(rows[i], index + 1, axis=1) - f * share
                rows[i] = (jnp.where(both, 0.0, rows[i]) - f * x) - g * y
            outside = (lane < first) | (lane >= first + PANEL)
            rows[k] = jnp.where(outside | (lane <= first + k), upper, 0.0) * lax.rsqrt(p)
            rows[k + 1] = jnp.where(outside | (lane <= first + k + 1), lower, 0.0) * lax.sqrt(last)
        for i in range(PANEL):
            panel_ref[i] = rows[i]
        below = row_id >= first + PANEL
        inside = (col_id >= first) & (col_id < first + PANEL)
        for b in range(boxes):
            own = panel_ref[:, b, :]
            p_ref[b, pl.ds(first, PANEL), :] = jnp.where(col_id[:PANEL] <= row_id[:PANEL] + first, own, 0.0)
            w1, w2, w3 = parts(own, 3)
            left = jnp.concatenate([w1, w1, w2, w1, w2, w3], 0)
            right = jnp.concatenate([w1, w2, w1, w3, w2, w1], 0)
            update = lax.dot_general(left, right, TN, preferred_element_type=jnp.float32)
            old = a_ref[b]
            a_ref[b] = jnp.where(below, jnp.where(inside, 0.0, old) - update, old)
        return carry

    lax.fori_loop(0, rank // PANEL, panel, 0)


def block_of(t, own):
    marks = [t // 40, (t + 22) // 72, (t + 20) // 72, (t + 12) // 72]
    p = t % 10
    some, last = (p + 6) // 10, (p + 3) // 10
    c, x = p - 4 * some - 2 * last, some - 2 * last
    r = t // 20
    steps = [(r, c, t % 20 // 10 * (1 - 2 * r), x), (1 - own, c, 1 - 2 * own, x)]
    n = t - 50
    steps.append((1 - own, 3 * n, 1 - 2 * own, 2 * n - 1))
    n = t - 52
    r, right = n // 4, n // 2 % 2
    steps.append((r, 3 * right, n % 2 * (1 - 2 * r), 2 * right - 1))
    n = t - 60
    steps.append((own, n // 3, 2 * own - 1, n % 3 - 1))
    r, c, y, x = steps[0]
    for mark, before, after in zip(marks, steps, steps[1:]):
        r, c, y, x = [now + mark * (b - a) for now, a, b in zip((r, c, y, x), before, after)]
    return r * TILE + c, 3 * (y + 1) + x + 1


def full_gram(value):
    a, b, c = parts(value, 3)
    rank = value.shape[1]
    wide = lax.dot_general(a, jnp.concatenate([a, b], 1), TN, preferred_element_type=jnp.float32)
    rest = lax.dot_general(
        jnp.concatenate([a, b], 0), jnp.concatenate([c, b * 0.5], 0), TN, preferred_element_type=jnp.float32
    )
    cross = wide[:, rank:] + rest
    return wide[:, :rank] + (cross + cross.T)


def full_apply(value, factor):
    a, b, c = parts(value, 3)
    p, q, r = parts(factor, 3)
    rank = value.shape[1]
    right = jnp.concatenate([jnp.concatenate([p, p], 1), jnp.concatenate([q, q], 1)], 0)
    wide = lax.dot_general(jnp.concatenate([a, b], 1), right, NT, preferred_element_type=jnp.float32)
    rest = lax.dot_general(
        jnp.concatenate([c, a], 1), jnp.concatenate([p, r], 1), NT, preferred_element_type=jnp.float32
    )
    return wide[:, :rank] + (wide[:, rank:] + rest)


def near_gram(value):
    a, b = parts(value, 2)
    rank = value.shape[1]
    wide = lax.dot_general(a, jnp.concatenate([a, b], 1), TN, preferred_element_type=jnp.float32)
    cross = wide[:, rank:]
    return wide[:, :rank] + (cross + cross.T)


def near_apply(value, factor):
    a, b = parts(value, 2)
    p, q = parts(factor, 2)
    rank = value.shape[1]
    right = jnp.concatenate([jnp.concatenate([p, p], 1), jnp.concatenate([q, jnp.zeros_like(q)], 1)], 0)
    wide = lax.dot_general(jnp.concatenate([a, b], 1), right, NT, preferred_element_type=jnp.float32)
    return wide[:, :rank] + wide[:, rank:]


def kernel(
    plate, mask_ref, points_ref, sketch_ref, basis_ref, coupling_ref,
    ext_p, ext_e, ext_o, ext_b, ext_d, rough, kbuf, even, odd, turned, y_ref, work, a_ref, p_ref, panel_ref, scale_ref, basis_t, stage,
    local_sem, out_sem, swap_send, swap_recv, p_send, p_recv, o_send, o_recv,
    b_send, b_recv, d_send, d_recv, half_send, half_recv, c_send, c_recv,
):
    halo = Halo(plate)
    own, other = halo.col, 1 - halo.col
    half = sketch_ref.shape[1]
    rank_half = coupling_ref.shape[2]
    inner = slice(1, TILE + 1)
    mine = pl.ds(pl.multiple_of(own * half, half), half)
    theirs = pl.ds(pl.multiple_of(other * half, half), half)
    locals_p, locals_o, swaps = [], [], []
    for r in range(2):
        boxes = pl.ds(own * 8 + r * TILE, TILE)
        away = pl.ds(other * 8 + r * TILE, TILE)
        locals_p.append(pltpu.make_async_copy(points_ref.at[boxes], ext_p.at[1 + r, inner], local_sem.at[r]))
        locals_o.append(
            pltpu.make_async_copy(sketch_ref.at[boxes], ext_o.at[1 + r, inner, mine], local_sem.at[2 + r])
        )
        swaps.append(
            pltpu.make_async_remote_copy(
                src_ref=sketch_ref.at[away],
                dst_ref=ext_o.at[1 + r, inner, mine],
                send_sem=swap_send.at[r],
                recv_sem=swap_recv.at[r],
                device_id=halo.partner,
                device_id_type=MESH,
            )
        )
    for copy in locals_p + locals_o:
        copy.start()
    halo.barrier()
    for copy in swaps:
        copy.start()
    for copy in locals_p:
        copy.wait()
    p_copies = halo.copies(ext_p, 1, ext_p, p_send, p_recv)
    for copy in p_copies:
        copy.start()

    def own_features(b, carry):
        r, c = 1 + b // TILE, 1 + b % TILE
        value = features(ext_p[r, c])
        ext_e[r, c] = value
        turned[b] = jnp.transpose(value)
        return carry

    lax.fori_loop(0, 8, own_features, 0)
    for copy in locals_o:
        copy.wait()
    for copy in swaps:
        copy.wait_recv()
    o_copies = halo.copies(ext_o, 1, ext_o, o_send, o_recv)
    for copy in o_copies:
        copy.start()

    def weight_of(b, slot):
        return mask_ref[own * 8 + b, slot].astype(jnp.float32)

    def first_term(b, carry):
        y_ref[b] = ext_o[1 + b // TILE, 1 + b % TILE].astype(jnp.float32) * weight_of(b, 4)
        return carry

    lax.fori_loop(0, 8, first_term, 0)

    def fill_block(t, copy_ref):
        b, slot = block_of(t, own)
        near = ext_e[b // TILE + slot // 3, b % TILE + slot % 3]
        u = near[0:1] + (slot % 3 - 1) * SCALE
        v = near[1:2] + (slot // 3 - 1) * SCALE
        h = near[2:3]
        norm = u * u + v * v + h * h + 4.0
        u, v, h = -2.0 * u, -2.0 * v, -2.0 * h
        step = 64
        for first in range(0, POINTS, step):
            rows = slice(first, first + step)
            own_rows = turned[b, rows, :]
            square = (own_rows[:, 3:4] + norm) + own_rows[:, 0:1] * u
            square = square + (own_rows[:, 1:2] * v + own_rows[:, 2:3] * h)
            values = lax.rsqrt(square).astype(jnp.bfloat16)
            kbuf[b, slot, rows, :] = values
            copy_ref[rows, :] = values

    def add_block(t, copy_ref):
        b, slot = block_of(t, own)
        near = ext_o[b // TILE + slot // 3, b % TILE + slot % 3]
        y_ref[b] += jnp.dot(copy_ref[...], near, preferred_element_type=jnp.float32) * weight_of(b, slot)

    def sketch_pair(i, carry):
        t = 2 * i
        add_block(t, even)
        fill_block(t + 1, odd)
        add_block(t + 1, odd)
        fill_block(jnp.minimum(t + 2, 71), even)
        return carry

    def couple_blocks(blocks, mirrored=False, batched=False):
        moved = []
        for b, slot in blocks:
            value = jnp.dot(basis_t[b], kbuf[b, slot], preferred_element_type=jnp.float32)
            moved.append(value.astype(jnp.bfloat16))
        turned_blocks = []
        for (b, slot), value in zip(blocks, moved):
            y, x = slot // 3 - 1, slot % 3 - 1
            near = ext_b[b // TILE + 1 + y, b % TILE + 1 + x]
            value = jnp.dot(value, near, preferred_element_type=jnp.float32) * (1.0 / POINTS)
            stage[b, slot] = (value * weight_of(b, slot)).astype(stage.dtype)
            if mirrored:
                other_b = b + TILE * y + x
                stage[other_b, 8 - slot] = (value.T * weight_of(other_b, 8 - slot)).astype(stage.dtype)
                turned_blocks.append((other_b, 8 - slot))
        for done in (blocks, turned_blocks):
            if batched and done:
                start_out(done[0][0], done[0][1], len(done))
            for b, slot in [] if batched else done:
                start_out(b, slot, 1)

    def start_out(b, slot, count):
        keep, give = out_copies(pl.ds(b, count), pl.ds(slot, 1), own * 8 + b, count)
        keep.start()
        give.start()

    def out_copies(b, slot, first, count):
        kept = pl.ds(pl.multiple_of(own * rank_half, rank_half), rank_half)
        given = pl.ds(pl.multiple_of(other * rank_half, rank_half), rank_half)
        target = coupling_ref.at[pl.ds(first, count), slot]
        keep = pltpu.make_async_copy(stage.at[b, slot, kept], target, out_sem)
        give = pltpu.make_async_remote_copy(
            src_ref=stage.at[b, slot, given],
            dst_ref=target,
            send_sem=c_send,
            recv_sem=c_recv,
            device_id=halo.partner,
            device_id_type=MESH,
        )
        return keep, give

    fill_block(0, even)
    lax.fori_loop(0, 19, sketch_pair, 0)
    for copy in p_copies:
        copy.wait_recv()

    def halo_features(t, carry):
        r, c = t // 6, t % 6
        ext_e[3 * r, c] = features(ext_p[3 * r, c])
        return carry

    lax.fori_loop(0, 12, halo_features, 0)

    def side_features(t, carry):
        r, c = 1 + t // 2, t % 2 * (TILE + 1)
        ext_e[r, c] = features(ext_p[r, c])
        return carry

    lax.fori_loop(0, 4, side_features, 0)
    await_row(halo, True, ext_o, o_send, o_recv)
    lax.fori_loop(19, 25, sketch_pair, 0)
    for copy in o_copies[3:5]:
        copy.wait_recv()
    lax.fori_loop(25, 30, sketch_pair, 0)
    await_row(halo, False, ext_o, o_send, o_recv)
    lax.fori_loop(30, 36, sketch_pair, 0)

    def add_units(b, carry):
        same = lax.broadcasted_iota(jnp.int32, (128, 128), 0) == lax.broadcasted_iota(jnp.int32, (128, 128), 1)
        unit = jnp.where(same, 1.0, 0.0)
        for first in range(0, POINTS, 128):
            part = slice(first, first + 128)
            kbuf[b, 4, part, part] = (kbuf[b, 4, part, part].astype(jnp.float32) + unit).astype(jnp.bfloat16)
        return carry


    def by_fours(step):
        def four(i, carry):
            for n in range(4):
                step(4 * i + n, carry)
            return carry

        lax.fori_loop(0, 2, four, 0)

    def first_gram(b, carry):
        value = y_ref[b]
        gram = full_gram(value)
        at = [lax.broadcasted_iota(jnp.int32, (RANK, RANK), axis) for axis in (0, 1)]
        diagonal = jnp.where(at[0] == at[1], gram, 0.0)
        along, across = [lax.rsqrt(jnp.sum(diagonal, axis=axis, keepdims=True)) for axis in (0, 1)]
        a_ref[b] = gram * along * across
        scale_ref[b] = jnp.broadcast_to(along * math.sqrt(POINTS), (8, RANK))
        return carry

    def first_apply(b, carry):
        value = full_apply(y_ref[b], p_ref[b] * scale_ref[b, 0:1])
        work[b] = value
        rough[b // TILE, b % TILE] = value.astype(jnp.bfloat16)
        return carry

    def second_gram(b, carry):
        a_ref[b] = near_gram(work[b]) * (1.0 / POINTS)
        return carry

    def second_apply(b, carry):
        value = near_apply(work[b], p_ref[b])
        ext_b[1 + b // TILE, 1 + b % TILE] = value.astype(jnp.bfloat16)
        return carry

    by_fours(first_gram)
    eliminate(a_ref, p_ref, panel_ref)
    b_copies = []
    for near_core in (False, True):

        def apply_row(n, carry, row=1 - own if near_core else own):
            for m in range(2):
                first_apply(row * TILE + 2 * n + m, carry)
            return carry

        lax.fori_loop(0, 2, apply_row, 0)
        started = row_copies(halo, near_core, rough, ext_b, b_send, b_recv)
        for copy in started:
            copy.start()
        b_copies += started
    sides = halo.copies(rough, 0, ext_b, b_send, b_recv)[3:5]
    for copy in sides:
        copy.start()
    b_copies += sides
    lax.fori_loop(0, 8, add_units, 0)
    by_fours(second_gram)
    eliminate(a_ref, p_ref, panel_ref)

    def step_of(b, carry):
        at = [lax.broadcasted_iota(jnp.int32, (RANK, RANK), axis) for axis in (0, 1)]
        step = p_ref[b] - jnp.where(at[0] == at[1], 1.0, 0.0)
        ext_d[1 + b // TILE, 1 + b % TILE] = step.astype(jnp.bfloat16)
        return carry

    lax.fori_loop(0, 8, step_of, 0)
    by_fours(second_apply)
    d_copies = halo.copies(ext_d, 1, ext_d, d_send, d_recv)
    for copy in d_copies:
        copy.start()

    def turn_basis(b, carry):
        value = ext_b[1 + b // TILE, 1 + b % TILE].astype(jnp.float32)
        basis_t[b] = jnp.transpose(value).astype(jnp.bfloat16)
        return carry

    lax.fori_loop(0, 8, turn_basis, 0)
    keeps, gives = [], []
    for r in range(2):
        boxes = pl.ds(own * 8 + r * TILE, TILE)
        keeps.append(
            pltpu.make_async_copy(ext_b.at[1 + r, inner, mine], basis_ref.at[boxes], local_sem.at[r])
        )
        gives.append(
            pltpu.make_async_remote_copy(
                src_ref=ext_b.at[1 + r, inner, theirs],
                dst_ref=basis_ref.at[boxes],
                send_sem=half_send.at[r],
                recv_sem=half_recv.at[r],
                device_id=halo.partner,
                device_id_type=MESH,
            )
        )
    for copy in keeps + gives:
        copy.start()

    def couple_centres(i, carry):
        couple_blocks([(4 * i + n, 4) for n in range(4)], batched=True)
        return carry

    lax.fori_loop(0, 2, couple_centres, 0)
    for n, pairs in enumerate(PAIRS):
        couple_blocks(pairs, mirrored=True, batched=n == 0)

    def couple_across(r, y):
        def body(i, carry):
            couple_blocks([(r * TILE + n, 3 * (y + 1) + i) for n in range(4)], batched=True)
            return carry

        lax.fori_loop(0, 3, body, 0)

    def couple_sides(right, carry):
        couple_blocks([(n // 2 * TILE + 3 * right, 3 * (n % 2 * (1 - n // 2 * 2) + 1) + 2 * right) for n in range(4)])
        return carry

    def finish_near(r, c):
        near = ext_b[r, c]
        change = lax.dot_general(near, ext_d[r, c], NT, preferred_element_type=jnp.float32)
        ext_b[r, c] = (near.astype(jnp.float32) + change).astype(jnp.bfloat16)

    def finish_row(row):
        def finish(c, carry):
            finish_near(row, c)
            return carry

        lax.fori_loop(0, TILE + 2, finish, 0)

    def finish_side(t, carry):
        finish_near(1 + t // 2, t % 2 * (TILE + 1))
        return carry

    await_row(halo, True, ext_b, b_send, b_recv)
    await_row(halo, True, ext_d, d_send, d_recv)
    for copy in sides + d_copies[3:5]:
        copy.wait_recv()
    finish_row(3 * (1 - own))
    lax.fori_loop(0, 4, finish_side, 0)
    couple_across(1 - own, 1 - 2 * own)
    lax.fori_loop(0, 2, couple_sides, 0)
    await_row(halo, False, ext_b, b_send, b_recv)
    await_row(halo, False, ext_d, d_send, d_recv)
    finish_row(3 * own)
    couple_across(own, 2 * own - 1)
    keep, give = out_copies(slice(None), slice(None), own * 8, 8)
    keep.wait()
    give.wait()
    for copy in keeps + gives:
        copy.wait()
    for copy in swaps + p_copies + o_copies + b_copies + d_copies:
        copy.wait_send()


def body(plate, points, sketch, near_mask):
    boxes = points.shape[0]
    mine = boxes // 2
    hbm, smem = (pl.BlockSpec(memory_space=space) for space in (pl.ANY, pltpu.SMEM))
    dma = pltpu.SemaphoreType.DMA
    columns = pltpu.VMEM((4, TILE + 2, POINTS, RANK), jnp.bfloat16)
    tall = pltpu.VMEM((mine, POINTS, RANK), jnp.float32)
    square = pltpu.VMEM((mine, RANK, RANK), jnp.float32)
    basis, coupling = pl.pallas_call(
        functools.partial(kernel, plate),
        out_shape=(
            jax.ShapeDtypeStruct((boxes, POINTS // 2, RANK), jnp.bfloat16),
            jax.ShapeDtypeStruct((boxes, SLOTS, RANK // 2, RANK), jnp.bfloat16),
        ),
        in_specs=[smem, hbm, hbm],
        out_specs=(hbm, hbm),
        scratch_shapes=[
            pltpu.VMEM((4, TILE + 2, 3, POINTS), jnp.bfloat16),
            pltpu.VMEM((4, TILE + 2, FEATURES, POINTS), jnp.float32),
            columns, columns,
            pltpu.VMEM((4, TILE + 2, RANK, RANK), jnp.bfloat16),
            pltpu.VMEM((2, TILE, POINTS, RANK), jnp.bfloat16),
            pltpu.VMEM((mine, SLOTS, POINTS, POINTS), jnp.bfloat16),
            pltpu.VMEM((POINTS, POINTS), jnp.bfloat16),
            pltpu.VMEM((POINTS, POINTS), jnp.bfloat16),
            pltpu.VMEM((mine, POINTS, FEATURES), jnp.float32),
            tall, tall, square, square,
            pltpu.VMEM((PANEL, mine, RANK), jnp.float32),
            pltpu.VMEM((mine, 8, RANK), jnp.float32),
            pltpu.VMEM((mine, RANK, POINTS), jnp.bfloat16),
            pltpu.VMEM((mine, SLOTS, RANK, RANK), jnp.bfloat16),
            dma((4,)), dma, dma((2,)), dma((2,)), dma((8,)), dma((8,)), dma((8,)), dma((8,)),
            dma((8,)), dma((8,)), dma((8,)), dma((8,)), dma((2,)), dma((2,)), dma, dma,
        ],
        compiler_params=pltpu.CompilerParams(collective_id=0, has_side_effects=True, vmem_limit_bytes=LIMIT),
        name="plate_level",
    )(near_mask, points, sketch)
    return basis, coupling.astype(jnp.float32)


def solution(mesh):
    plate = math.isqrt(mesh.shape["box"])

    def step(points, sketch, near_mask):
        return body(plate, points, sketch, near_mask)

    return jax.shard_map(
        step,
        mesh=mesh,
        in_specs=(P("box", None, None), P("box", "col", None), P("box", None)),
        out_specs=(P("box", "col", None), P("box", None, "col", None)),
        check_vma=False,
    )
```
